32 devices in a mesh: grp: 2 (over x), limb: 16 (over z, y, core).
Axes of the slice: x: 2, y: 2, z: 4, core: 2. Of those that a mesh axis runs over, the one named last changes fastest.
Arguments:
- digits: float32 [8, 3, 16, 65536], P('grp', None, None, 'limb'), may hold values from 0 to 2047, as said below
- keys: float32 [8, 3, 2, 16, 65536], P('grp', None, None, None, 'limb'), may hold values from 0 to 2047, as said below
- requests: int32 [8, 8], P('grp'), may hold values from 0 to 1, as said below
- rotations: int32 [8], replicated, may hold values from 1 to 256, as said below
- moduli: int32 [16], replicated, may hold values from 2048 to 4095
Outputs:
- switched: float32 [8, 2, 16, 65536], P('grp', None, None, 'limb')
The draws below stay inside these ranges and needn't reach their ends.
Inputs may be any that keep to these rules, and one draw needn't show every extreme that they name: `digits`: every entry is an integer. `keys`: every entry is an integer. `requests`: for each block of ciphertexts k * 4 to (k + 1) * 4 - 1 and each owner group's keys g * 4 to (g + 1) * 4 - 1, between 1 and 2 of those ciphertexts request one or more of those keys; in every draw some owner group is requested by exactly 2 ciphertexts of every block. `rotations`: the largest amount is exactly 256.
All inputs are finite; a program needn't handle non-finite values.
Results may differ from the reference program's by a relative error of at most 0.0003.
Values sent between devices are 32-bit elements; how exact they have to be, the bound alone decides.
No kernel may reach another device: no remote copies, remote signals or barrier semaphores. Data moves between devices by JAX's collectives and lax.ppermute only.
A program may use at most 64 MiB of HBM per device.

```python
import jax
import jax.numpy as jnp
from jax import lax

NCOEF = 65536
DNUM = 3
LIMBS = 16
KEYS_GRP = 4
RMAX = 256
CT_GRP = 4
CAP = 2
CTS = 8
KEYS = 8


def draw_digits(key, part):
    return jax.random.randint(key, (CTS, DNUM, LIMBS, NCOEF), 0, 2048).astype(jnp.float32)


def draw_keys(key, part):
    return jax.random.randint(key, (KEYS, DNUM, 2, LIMBS, NCOEF), 0, 2048).astype(jnp.float32)


def draw_requests(key, part):
    groups = CTS // CT_GRP
    count_key, busy_key, score_key, subset_key = jax.random.split(key, 4)
    counts = jax.random.randint(count_key, (groups, groups), 1, CAP + 1)
    busiest = jax.random.randint(busy_key, (), 0, groups)
    counts = jnp.where(jnp.arange(groups)[None, :] == busiest, CAP, counts)
    scores = jax.random.randint(score_key, (groups, groups, CT_GRP), 0, 1048576) * CT_GRP + jnp.arange(CT_GRP)
    ranking = jnp.argsort(jnp.argsort(scores, axis=2, stable=True), axis=2, stable=True)
    chosen = (ranking < counts[:, :, None]).astype(jnp.int32)
    subsets = jax.random.randint(subset_key, (groups, groups, CT_GRP), 1, 2 ** KEYS_GRP)
    powers = 2 ** jnp.arange(KEYS_GRP)
    key_bits = subsets[..., None] // powers % 2
    request = chosen[..., None] * key_bits
    return jnp.transpose(request, (0, 2, 1, 3)).reshape(CTS, KEYS).astype(jnp.int32)


def draw_rotations(key, part):
    amount_key, place_key = jax.random.split(key)
    amounts = jax.random.randint(amount_key, (KEYS,), 1, RMAX + 1)
    largest_at = jax.random.randint(place_key, (), 0, KEYS)
    return jnp.where(jnp.arange(KEYS) == largest_at, RMAX, amounts).astype(jnp.int32)


def draw_moduli(key, part):
    return jax.random.randint(key, (LIMBS,), 2048, 4096).astype(jnp.int32)


def setup_inputs(seed: int = 0) -> dict:
    splits = jax.random.split(jax.random.key(seed), 6)
    digits = draw_digits(jax.random.fold_in(splits[5], 71), 0)
    keys = draw_keys(jax.random.fold_in(splits[5], 71), 0)
    requests = draw_requests(jax.random.fold_in(splits[5], 71), 0)
    rotations = draw_rotations(jax.random.fold_in(splits[5], 71), 0)
    moduli = draw_moduli(jax.random.fold_in(splits[5], 71), 0)
    return {"digits": digits, "keys": keys, "requests": requests, "rotations": rotations, "moduli": moduli}


def reduce_mod(amount, modulus):
    quotient = jnp.floor(amount * (1.0 / modulus))
    remainder = amount - quotient * modulus
    remainder = jnp.where(remainder < 0, remainder + modulus, remainder)
    return jnp.where(remainder >= modulus, remainder - modulus, remainder)


def reference(digits, keys, requests, rotations, moduli):
    modulus = moduli.astype(jnp.float32)[:, None]

    def one_cipher(operands):
        cipher_digits, wanted = operands

        def add_key(running, scanned):
            key_block, amount, wanted_flag = scanned
            combined = jnp.sum(cipher_digits[:, None] * key_block, axis=0)
            product = reduce_mod(combined, modulus)
            rotated = jnp.roll(product, -2 * amount, axis=-1)
            return running + wanted_flag.astype(jnp.float32) * rotated, None

        initial = jnp.zeros((2, LIMBS, NCOEF), jnp.float32)
        running, unused = lax.scan(add_key, initial, (keys, rotations, wanted))
        return reduce_mod(running, modulus) / modulus

    return lax.map(one_cipher, (digits, requests))
```

```python
import functools

import jax
import jax.numpy as jnp
from jax import lax
from jax.experimental import pallas as pl
from jax.experimental.pallas import tpu as pltpu
from jax.sharding import PartitionSpec as P

RMAX = 256
CAP = 2
WIDEST = 2 * RMAX
LANES = 128
ROWS = 8


def shifted(value, axis, steps):
    count = lax.axis_size(axis)
    pairs = [(source, (source + steps) % count) for source in range(count)]
    return lax.ppermute(value, axis, pairs)


def slot_ciphers(requests, ciphers, key_count, owner):
    needed = []
    for cipher in range(ciphers):
        flag = requests[cipher, owner * key_count]
        for key in range(1, key_count):
            flag = flag | requests[cipher, owner * key_count + key]
        needed.append(flag)
    slots = [jnp.int32(0)] * CAP
    rank = jnp.int32(0)
    for want in (1, 0):
        for cipher in range(ciphers):
            here = needed[cipher] == want
            for slot in range(CAP):
                slots[slot] = jnp.where(here & (rank == slot), cipher, slots[slot])
            rank = rank + here.astype(jnp.int32)
    return slots


def gather_kernel(slot, ciphers, key_count, requests, owner, digits, out, held, in_sems, out_sems):
    cipher = slot_ciphers(requests, ciphers, key_count, owner[0])[slot]
    parts = held.shape[0]
    loads = [pltpu.make_async_copy(digits.at[cipher, j], held.at[j], in_sems.at[j]) for j in range(parts)]
    stores = [pltpu.make_async_copy(held.at[j], out.at[j], out_sems.at[j]) for j in range(parts)]
    for load in loads:
        load.start()
    for load, store in zip(loads, stores):
        load.wait()
        store.start()
    for store in stores:
        store.wait()


def gather_slot(digits, requests, owner, slot):
    ciphers, parts, limbs, columns = digits.shape
    key_count = requests.shape[1] // lax.axis_size("grp")
    return pl.pallas_call(
        functools.partial(gather_kernel, slot, ciphers, key_count),
        out_shape=jax.ShapeDtypeStruct((parts, limbs, columns), jnp.float32),
        in_specs=[
            pl.BlockSpec(memory_space=pltpu.SMEM),
            pl.BlockSpec(memory_space=pltpu.SMEM),
            pl.BlockSpec(memory_space=pl.ANY),
        ],
        out_specs=pl.BlockSpec(memory_space=pl.ANY),
        scratch_shapes=[
            pltpu.VMEM((parts, limbs, columns), jnp.float32),
            pltpu.SemaphoreType.DMA((parts,)),
            pltpu.SemaphoreType.DMA((parts,)),
        ],
        cost_estimate=pl.CostEstimate(flops=0, transcendentals=0, bytes_accessed=8 * parts * limbs * columns),
        name="gather_digits",
    )(requests, owner, digits)


def products_kernel(slots, digit_parts, ciphers, key_count, local, requests, owner, rotations, *refs):
    digit_refs = refs[: len(slots)]
    keys, modulus_ref = refs[len(slots) : len(slots) + 2]
    tail, resident, rolled = refs[len(slots) + 2 :]
    key = pl.program_id(1)
    columns = resident.shape[-1]
    pad = WIDEST // LANES
    tiles = columns // LANES

    @pl.when(key == 0)
    def _():
        tail[...] = jnp.zeros_like(tail)
        resident[...] = jnp.zeros_like(resident)
        rolled[...] = jnp.zeros_like(rolled)

    amount = 2 * rotations[owner[0] * key_count + key]
    skipped = amount // LANES
    within = amount - skipped * LANES
    turn = lax.rem(LANES - within, LANES)
    modulus = modulus_ref[...]
    inverse = 1.0 / modulus
    lane = lax.broadcasted_iota(jnp.int32, (ROWS, LANES), 1)
    from_this = lane < LANES - within
    chosen = slot_ciphers(requests, ciphers, key_count, owner[0])

    for place, slot in enumerate(slots):
        mark = requests[chosen[slot], owner[0] * key_count + key]

        @pl.when(mark > 0)
        def _():
            for poly in range(2):
                for tile in range(tiles):
                    at = pl.ds(tile * LANES, LANES)
                    combined = digit_refs[place][0, :, at] * keys[0, poly, :, at]
                    for part in range(1, digit_parts):
                        combined = combined + digit_refs[place][part, :, at] * keys[part, poly, :, at]
                    quotient = jnp.floor(combined * inverse)
                    remainder = combined - quotient * modulus
                    rolled[:, pl.ds((pad + tile) * LANES, LANES)] = pltpu.roll(remainder, turn, 1)
                for tile in range(pad + tiles):
                    start = pl.multiple_of((skipped + tile) * LANES, LANES)
                    after = pl.multiple_of((skipped + tile + 1) * LANES, LANES)
                    moved = jnp.where(from_this, rolled[:, pl.ds(start, LANES)], rolled[:, pl.ds(after, LANES)])
                    if tile < pad:
                        at = pl.ds(tile * LANES, LANES)
                        tail[place, poly, :, at] = tail[place, poly, :, at] + moved
                    else:
                        at = pl.ds((tile - pad) * LANES, LANES)
                        resident[place, poly, :, at] = resident[place, poly, :, at] + moved


def products(digits, keys, requests, owner, rotations, modulus, slots, local):
    key_count, parts, polys, limbs, columns = keys.shape
    ciphers = requests.shape[0]
    count = len(slots)
    pad = WIDEST // LANES

    if local:
        def digit_spec(slot):
            def index(block, key, requests, owner, rotations):
                return (slot_ciphers(requests, ciphers, key_count, owner[0])[slot], 0, block, 0)
            return pl.BlockSpec((pl.Squeezed(), parts, ROWS, columns), index)
        digit_specs = [digit_spec(slot) for slot in slots]
        digit_args = [digits] * count
    else:
        digit_specs = [pl.BlockSpec((parts, ROWS, columns), lambda block, key, *_: (0, block, 0))] * count
        digit_args = list(digits)
    tail_shape = (count, polys, limbs, WIDEST)
    resident_shape = (count, polys, limbs, columns)
    work = count * key_count * polys * limbs * columns
    return pl.pallas_call(
        functools.partial(products_kernel, slots, parts, ciphers, key_count, local),
        out_shape=[
            jax.ShapeDtypeStruct(tail_shape, jnp.float32),
            jax.ShapeDtypeStruct(resident_shape, jnp.float32),
        ],
        grid_spec=pltpu.PrefetchScalarGridSpec(
            num_scalar_prefetch=3,
            grid=(limbs // ROWS, key_count),
            in_specs=digit_specs
            + [
                pl.BlockSpec(
                    (pl.Squeezed(), parts, polys, ROWS, columns), lambda block, key, *_: (key, 0, 0, block, 0)
                ),
                pl.BlockSpec((ROWS, LANES), lambda block, key, *_: (block, 0)),
            ],
            out_specs=[
                pl.BlockSpec((count, polys, ROWS, WIDEST), lambda block, key, *_: (0, 0, block, 0)),
                pl.BlockSpec((count, polys, ROWS, columns), lambda block, key, *_: (0, 0, block, 0)),
            ],
            scratch_shapes=[pltpu.VMEM((ROWS, columns + 2 * pad * LANES + LANES), jnp.float32)],
        ),
        compiler_params=pltpu.CompilerParams(dimension_semantics=("arbitrary", "arbitrary")),
        cost_estimate=pl.CostEstimate(
            flops=20 * work, transcendentals=0, bytes_accessed=4 * (keys.size + count * limbs * columns * (parts + polys))
        ),
        name="products",
    )(requests, owner, rotations, *digit_args, keys, modulus)


def add_tail_kernel(arrived, held, out):
    out[...] = held[...] + arrived[...]


def add_tail(resident, arrived):
    count, polys, limbs, columns = resident.shape
    last = columns // WIDEST - 1
    here = pl.BlockSpec((count, polys, limbs, WIDEST), lambda i: (0, 0, 0, last))
    return pl.pallas_call(
        add_tail_kernel,
        out_shape=jax.ShapeDtypeStruct(resident.shape, jnp.float32),
        grid=(1,),
        in_specs=[pl.BlockSpec((count, polys, limbs, WIDEST), lambda i: (0, 0, 0, 0)), here],
        out_specs=here,
        input_output_aliases={1: 0},
        name="add_tail",
    )(arrived, resident)


def reduce_mod(amount, modulus):
    quotient = jnp.floor(amount * (1.0 / modulus))
    remainder = amount - quotient * modulus
    remainder = jnp.where(remainder < 0, remainder + modulus, remainder)
    return jnp.where(remainder >= modulus, remainder - modulus, remainder)


def gather_sums_kernel(owners, groups, ciphers, key_count, requests, me, modulus, *refs):
    parts = refs[: len(owners)]
    out, held = refs[len(owners) :]
    cipher = pl.program_id(1)
    out[...] = jnp.zeros_like(out)
    for part, (steps, slots) in zip(parts, owners):
        owner = lax.rem(me[0] + steps, groups)
        chosen = slot_ciphers(requests, ciphers, key_count, owner)
        for place, slot in enumerate(slots):

            @pl.when(chosen[slot] == cipher)
            def _():
                out[...] = out[...] + part[place]

    last = slot_ciphers(requests, ciphers, key_count, lax.rem(me[0] + groups - 1, groups))[CAP - 1]

    @pl.when(cipher == last)
    def _():
        held[...] = out[...]

    wide = modulus[:, :1]
    out[...] = reduce_mod(out[...], wide) / wide


def gather_sums(parts, owners, requests, me, modulus, ciphers):
    polys, limbs, columns = parts[0].shape[1:]
    groups = lax.axis_size("grp")
    key_count = requests.shape[1] // groups
    return pl.pallas_call(
        functools.partial(gather_sums_kernel, owners, groups, ciphers, key_count),
        out_shape=[
            jax.ShapeDtypeStruct((ciphers, polys, limbs, columns), jnp.float32),
            jax.ShapeDtypeStruct((polys, limbs, columns), jnp.float32),
        ],
        grid_spec=pltpu.PrefetchScalarGridSpec(
            num_scalar_prefetch=2,
            grid=(limbs // ROWS, ciphers),
            in_specs=[pl.BlockSpec((ROWS, LANES), lambda block, cipher, *_: (block, 0))]
            + [
                pl.BlockSpec((part.shape[0], polys, ROWS, columns), lambda block, cipher, *_: (0, 0, block, 0))
                for part in parts
            ],
            out_specs=[
                pl.BlockSpec((pl.Squeezed(), polys, ROWS, columns), lambda block, cipher, *_: (cipher, 0, block, 0)),
                pl.BlockSpec((polys, ROWS, columns), lambda block, cipher, *_: (0, block, 0)),
            ],
        ),
        compiler_params=pltpu.CompilerParams(dimension_semantics=("arbitrary", "arbitrary")),
        cost_estimate=pl.CostEstimate(
            flops=20 * ciphers * polys * limbs * columns,
            transcendentals=0,
            bytes_accessed=4 * (ciphers + 2 + 2 * len(parts)) * polys * limbs * columns,
        ),
        name="gather_sums",
    )(requests, me, modulus, *parts)


def last_slot_kernel(requests, me, modulus, part, held, before, out):
    wide = modulus[:, :1]
    out[...] = reduce_mod(held[...] + part[...], wide) / wide


def last_slot(part, held, result, requests, me, modulus):
    ciphers, polys, limbs, columns = result.shape
    groups = lax.axis_size("grp")
    key_count = requests.shape[1] // groups

    def place(poly, block, requests, me):
        owner = lax.rem(me[0] + groups - 1, groups)
        return (slot_ciphers(requests, ciphers, key_count, owner)[CAP - 1], poly, block, 0)

    return pl.pallas_call(
        last_slot_kernel,
        out_shape=jax.ShapeDtypeStruct(result.shape, jnp.float32),
        grid_spec=pltpu.PrefetchScalarGridSpec(
            num_scalar_prefetch=2,
            grid=(polys, limbs // ROWS),
            in_specs=[
                pl.BlockSpec((ROWS, LANES), lambda poly, block, *_: (block, 0)),
                pl.BlockSpec((pl.Squeezed(), pl.Squeezed(), ROWS, columns), lambda poly, block, *_: (0, poly, block, 0)),
                pl.BlockSpec((pl.Squeezed(), ROWS, columns), lambda poly, block, *_: (poly, block, 0)),
                pl.BlockSpec(memory_space=pl.ANY),
            ],
            out_specs=pl.BlockSpec((pl.Squeezed(), pl.Squeezed(), ROWS, columns), place),
        ),
        input_output_aliases={5: 0},
        compiler_params=pltpu.CompilerParams(dimension_semantics=("arbitrary", "arbitrary")),
        name="last_slot",
    )(requests, me, modulus, part, held, result)


def per_device(digits, keys, requests, rotations, moduli):
    groups = lax.axis_size("grp")
    ciphers = digits.shape[0]
    limbs = digits.shape[2]
    me = lax.axis_index("grp").astype(jnp.int32).reshape(1)
    modulus = jnp.broadcast_to(moduli.astype(jnp.float32)[:, None], (limbs, LANES))

    sent = {}
    asked = {}
    for steps in range(1, groups):
        owner = lax.rem(me + steps, groups)
        for slot in range(CAP):
            sent[steps, slot] = shifted(gather_slot(digits, requests, owner, slot), "grp", steps)
        asked[steps] = shifted(requests, "grp", steps)

    tail, resident = products(digits, keys, requests, me, rotations, modulus, tuple(range(CAP)), True)
    parts = [add_tail(resident, shifted(tail, "limb", -1))]
    owners = [(0, tuple(range(CAP)))]
    for steps in range(1, groups):
        for slot in range(CAP):
            tail, resident = products(
                [sent[steps, slot]], keys, asked[steps], me, rotations, modulus, (slot,), False
            )
            whole = add_tail(resident, shifted(tail, "limb", -1))
            parts.append(shifted(whole, "grp", -steps))
            owners.append((steps, (slot,)))
    result, held = gather_sums(parts[:-1], tuple(owners[:-1]), requests, me, modulus, ciphers)
    return last_slot(parts[-1], held, result, requests, me, modulus)


def solution(mesh):
    in_specs = (
        P("grp", None, None, "limb"),
        P("grp", None, None, None, "limb"),
        P("grp", None),
        P(),
        P(),
    )
    out_specs = P("grp", None, None, "limb")
    return jax.shard_map(
        per_device, mesh=mesh, in_specs=in_specs, out_specs=out_specs, check_vma=False
    )
```

```python
import functools

import jax
import jax.numpy as jnp
from jax import lax
from jax.experimental import pallas as pl
from jax.experimental.pallas import tpu as pltpu
from jax.sharding import PartitionSpec as P

RMAX = 256
CAP = 2
WIDEST = 2 * RMAX
LANES = 128
ROWS = 8
SMEM = pl.BlockSpec(memory_space=pltpu.SMEM)
VMEM = pl.BlockSpec(memory_space=pltpu.VMEM)


def shifted(value, axis, steps):
    count = lax.axis_size(axis)
    pairs = [(source, (source + steps) % count) for source in range(count)]
    return lax.ppermute(value, axis, pairs)


def slot_ciphers(requests, ciphers, key_count, owner):
    needed = []
    for cipher in range(ciphers):
        flag = requests[cipher, owner * key_count]
        for key in range(1, key_count):
            flag = flag | requests[cipher, owner * key_count + key]
        needed.append(flag)
    slots = [jnp.int32(0)] * CAP
    rank = jnp.int32(0)
    for want in (1, 0):
        for cipher in range(ciphers):
            here = needed[cipher] == want
            for slot in range(CAP):
                slots[slot] = jnp.where(here & (rank == slot), cipher, slots[slot])
            rank = rank + here.astype(jnp.int32)
    return slots


def gather_kernel(slot, ciphers, key_count, requests, owner, digits, out, sems):
    cipher = slot_ciphers(requests, ciphers, key_count, owner[0])[slot]
    loads = [pltpu.make_async_copy(digits.at[cipher, j], out.at[j], sems.at[j]) for j in range(out.shape[0])]
    for load in loads:
        load.start()
    for load in loads:
        load.wait()


def gather_slot(digits, requests, owner, slot):
    ciphers, parts, limbs, columns = digits.shape
    key_count = requests.shape[1] // lax.axis_size("grp")
    return pl.pallas_call(
        functools.partial(gather_kernel, slot, ciphers, key_count),
        out_shape=jax.ShapeDtypeStruct((parts, limbs, columns), jnp.float32),
        in_specs=[SMEM, SMEM, pl.BlockSpec(memory_space=pltpu.HBM)],
        out_specs=VMEM,
        scratch_shapes=[pltpu.SemaphoreType.DMA((parts,))],
        compiler_params=pltpu.CompilerParams(vmem_limit_bytes=4 << 20),
        cost_estimate=pl.CostEstimate(flops=0, transcendentals=0, bytes_accessed=8 * parts * limbs * columns),
        name="gather_digits",
    )(requests, owner, pltpu.with_memory_space_constraint(digits, pltpu.HBM))


def products_kernel(slots, local, requests, owner, rotations, digits, keys, modulus_ref, tail, resident, rolled):
    key_count, parts, polys, limbs, columns = keys.shape
    ciphers = requests.shape[0]
    pad = WIDEST // LANES
    tiles = columns // LANES
    tail[...] = jnp.zeros_like(tail)
    resident[...] = jnp.zeros_like(resident)
    rolled[...] = jnp.zeros_like(rolled)
    lane = lax.broadcasted_iota(jnp.int32, (ROWS, LANES), 1)
    chosen = slot_ciphers(requests, ciphers, key_count, owner[0])

    def add_key(step, carry):
        block = step // key_count
        key = step - block * key_count
        rows = pl.ds(pl.multiple_of(block * ROWS, ROWS), ROWS)
        amount = 2 * rotations[owner[0] * key_count + key]
        skipped = amount // LANES
        within = amount - skipped * LANES
        turn = lax.rem(LANES - within, LANES)
        from_this = lane < LANES - within
        modulus = modulus_ref[rows, :]
        inverse = 1.0 / modulus
        for place, slot in enumerate(slots):
            source = chosen[slot] if local else place

            @pl.when(requests[chosen[slot], owner[0] * key_count + key] > 0)
            def _():
                for poly in range(polys):
                    for tile in range(tiles):
                        at = pl.ds(tile * LANES, LANES)
                        combined = digits[source, 0, rows, at] * keys[key, 0, poly, rows, at]
                        for part in range(1, parts):
                            combined = combined + digits[source, part, rows, at] * keys[key, part, poly, rows, at]
                        quotient = jnp.floor(combined * inverse)
                        remainder = combined - quotient * modulus
                        rolled[:, pl.ds((pad + tile) * LANES, LANES)] = pltpu.roll(remainder, turn, 1)
                    for tile in range(pad + tiles):
                        start = pl.multiple_of((skipped + tile) * LANES, LANES)
                        after = pl.multiple_of((skipped + tile + 1) * LANES, LANES)
                        moved = jnp.where(from_this, rolled[:, pl.ds(start, LANES)], rolled[:, pl.ds(after, LANES)])
                        if tile < pad:
                            at = pl.ds(tile * LANES, LANES)
                            tail[place, poly, rows, at] = tail[place, poly, rows, at] + moved
                        else:
                            at = pl.ds((tile - pad) * LANES, LANES)
                            resident[place, poly, rows, at] = resident[place, poly, rows, at] + moved
        return carry

    lax.fori_loop(0, (limbs // ROWS) * key_count, add_key, 0)


def products(digits, keys, requests, owner, rotations, modulus, slots, local):
    key_count, parts, polys, limbs, columns = keys.shape
    count = len(slots)
    pad = WIDEST // LANES
    work = count * key_count * polys * limbs * columns
    return pl.pallas_call(
        functools.partial(products_kernel, slots, local),
        out_shape=[
            jax.ShapeDtypeStruct((count, polys, limbs, WIDEST), jnp.float32),
            jax.ShapeDtypeStruct((count, polys, limbs, columns), jnp.float32),
        ],
        in_specs=[SMEM, SMEM, SMEM, VMEM, VMEM, VMEM],
        out_specs=[VMEM, VMEM],
        scratch_shapes=[pltpu.VMEM((ROWS, columns + 2 * pad * LANES + LANES), jnp.float32)],
        compiler_params=pltpu.CompilerParams(vmem_limit_bytes=20 << 20),
        cost_estimate=pl.CostEstimate(
            flops=20 * work, transcendentals=0, bytes_accessed=4 * (keys.size + count * limbs * columns * (parts + polys))
        ),
        name="products",
    )(requests, owner, rotations, digits, keys, modulus)


def add_tail_kernel(arrived, held, out):
    columns = held.shape[-1]
    at = pl.ds(columns - WIDEST, WIDEST)
    out[:, :, :, at] = held[:, :, :, at] + arrived[...]


def add_tail(resident, arrived):
    return pl.pallas_call(
        add_tail_kernel,
        out_shape=jax.ShapeDtypeStruct(resident.shape, jnp.float32),
        in_specs=[VMEM, VMEM],
        out_specs=VMEM,
        input_output_aliases={1: 0},
        compiler_params=pltpu.CompilerParams(vmem_limit_bytes=8 << 20),
        name="add_tail",
    )(arrived, resident)


def reduce_mod(amount, modulus):
    quotient = jnp.floor(amount * (1.0 / modulus))
    remainder = amount - quotient * modulus
    remainder = jnp.where(remainder < 0, remainder + modulus, remainder)
    return jnp.where(remainder >= modulus, remainder - modulus, remainder)


def gather_sums_kernel(owners, groups, ciphers, key_count, requests, me, modulus, *refs):
    parts = refs[: len(owners)]
    out, held = refs[len(owners) :]
    cipher = pl.program_id(1)
    out[...] = jnp.zeros_like(out)
    for part, (steps, slots) in zip(parts, owners):
        owner = lax.rem(me[0] + steps, groups)
        chosen = slot_ciphers(requests, ciphers, key_count, owner)
        for place, slot in enumerate(slots):

            @pl.when(chosen[slot] == cipher)
            def _():
                out[...] = out[...] + part[place]

    last = slot_ciphers(requests, ciphers, key_count, lax.rem(me[0] + groups - 1, groups))[CAP - 1]

    @pl.when(cipher == last)
    def _():
        held[...] = out[...]

    wide = modulus[:, :1]
    out[...] = reduce_mod(out[...], wide) / wide


def gather_sums(parts, owners, requests, me, modulus, ciphers):
    polys, limbs, columns = parts[0].shape[1:]
    groups = lax.axis_size("grp")
    key_count = requests.shape[1] // groups
    return pl.pallas_call(
        functools.partial(gather_sums_kernel, owners, groups, ciphers, key_count),
        out_shape=[
            jax.ShapeDtypeStruct((ciphers, polys, limbs, columns), jnp.float32),
            jax.ShapeDtypeStruct((polys, limbs, columns), jnp.float32),
        ],
        grid_spec=pltpu.PrefetchScalarGridSpec(
            num_scalar_prefetch=2,
            grid=(limbs // ROWS, ciphers),
            in_specs=[pl.BlockSpec((ROWS, LANES), lambda block, cipher, *_: (block, 0))]
            + [
                pl.BlockSpec((part.shape[0], polys, ROWS, columns), lambda block, cipher, *_: (0, 0, block, 0))
                for part in parts
            ],
            out_specs=[
                pl.BlockSpec((pl.Squeezed(), polys, ROWS, columns), lambda block, cipher, *_: (cipher, 0, block, 0)),
                pl.BlockSpec((polys, ROWS, columns), lambda block, cipher, *_: (0, block, 0)),
            ],
        ),
        compiler_params=pltpu.CompilerParams(dimension_semantics=("arbitrary", "arbitrary"), vmem_limit_bytes=12 << 20),
        cost_estimate=pl.CostEstimate(
            flops=20 * ciphers * polys * limbs * columns,
            transcendentals=0,
            bytes_accessed=4 * (ciphers + 2 + 2 * len(parts)) * polys * limbs * columns,
        ),
        name="gather_sums",
    )(requests, me, modulus, *parts)


def last_slot_kernel(groups, key_count, requests, me, modulus, part, held, before, out, done, sems):
    ciphers, polys, limbs, _ = out.shape
    cipher = slot_ciphers(requests, ciphers, key_count, lax.rem(me[0] + groups - 1, groups))[CAP - 1]
    stores = []
    for poly in range(polys):
        for block in range(limbs // ROWS):
            rows = pl.ds(block * ROWS, ROWS)
            wide = modulus[rows, :1]
            done[poly, rows, :] = reduce_mod(held[poly, rows, :] + part[0, poly, rows, :], wide) / wide
            store = pltpu.make_async_copy(
                done.at[poly, rows], out.at[cipher, poly, rows], sems.at[poly * (limbs // ROWS) + block]
            )
            store.start()
            stores.append(store)
    for store in stores:
        store.wait()


def last_slot(part, held, result, requests, me, modulus):
    _, polys, limbs, columns = result.shape
    groups = lax.axis_size("grp")
    key_count = requests.shape[1] // groups
    hbm = pl.BlockSpec(memory_space=pltpu.HBM)
    return pl.pallas_call(
        functools.partial(last_slot_kernel, groups, key_count),
        out_shape=jax.ShapeDtypeStruct(result.shape, jnp.float32),
        in_specs=[SMEM, SMEM, VMEM, VMEM, VMEM, hbm],
        out_specs=hbm,
        scratch_shapes=[
            pltpu.VMEM((polys, limbs, columns), jnp.float32),
            pltpu.SemaphoreType.DMA((polys * (limbs // ROWS),)),
        ],
        input_output_aliases={5: 0},
        compiler_params=pltpu.CompilerParams(vmem_limit_bytes=8 << 20),
        name="last_slot",
    )(requests, me, modulus, part, held, result)


def key_switch(digits, keys, requests, rotations, moduli):
    groups = lax.axis_size("grp")
    ciphers = digits.shape[0]
    limbs = digits.shape[2]
    me = lax.axis_index("grp").astype(jnp.int32).reshape(1)
    modulus = jnp.broadcast_to(moduli.astype(jnp.float32)[:, None], (limbs, LANES))
    turns = [(steps, slot) for steps in range(1, groups) for slot in range(CAP)]

    sent = {}
    asked = {}
    for steps, slot in turns:
        owner = lax.rem(me + steps, groups)
        picked = gather_slot(digits, requests, owner, slot)
        sent[steps, slot] = shifted(picked, "grp", steps)
        if slot == 0:
            asked[steps] = shifted(requests, "grp", steps)

    tail, resident = products(digits, keys, requests, me, rotations, modulus, tuple(range(CAP)), True)
    arrived = shifted(tail, "limb", -1)
    parts = [add_tail(resident, arrived)]
    owners = [(0, tuple(range(CAP)))]
    for steps, slot in turns:
        tail, resident = products(sent[steps, slot][None], keys, asked[steps], me, rotations, modulus, (slot,), False)
        arrived = shifted(tail, "limb", -1)
        whole = add_tail(resident, arrived)
        parts.append(shifted(whole, "grp", -steps))
        owners.append((steps, (slot,)))
    result, held = gather_sums(parts[:-1], tuple(owners[:-1]), requests, me, modulus, ciphers)
    return last_slot(parts[-1], held, result, requests, me, modulus)


def solution(mesh):
    in_specs = (
        P("grp", None, None, "limb"),
        P("grp", None, None, None, "limb"),
        P("grp", None),
        P(),
        P(),
    )
    out_specs = P("grp", None, None, "limb")
    return jax.shard_map(key_switch, mesh=mesh, in_specs=in_specs, out_specs=out_specs, check_vma=False)
```

```python
import functools

import jax
import jax.numpy as jnp
from jax import lax
from jax.experimental import pallas as pl
from jax.experimental.pallas import tpu as pltpu
from jax.sharding import PartitionSpec as P

RMAX = 256
CAP = 2
WIDEST = 2 * RMAX
LANES = 128
ROWS = 8
SMEM = pl.BlockSpec(memory_space=pltpu.SMEM)
VMEM = pl.BlockSpec(memory_space=pltpu.VMEM)


def shifted(value, axis, steps):
    count = lax.axis_size(axis)
    pairs = [(source, (source + steps) % count) for source in range(count)]
    return lax.ppermute(value, axis, pairs)


def slot_ciphers(requests, ciphers, key_count, owner):
    needed = []
    for cipher in range(ciphers):
        flag = requests[cipher, owner * key_count]
        for key in range(1, key_count):
            flag = flag | requests[cipher, owner * key_count + key]
        needed.append(flag)
    slots = [jnp.int32(0)] * CAP
    rank = jnp.int32(0)
    for want in (1, 0):
        for cipher in range(ciphers):
            here = needed[cipher] == want
            for slot in range(CAP):
                slots[slot] = jnp.where(here & (rank == slot), cipher, slots[slot])
            rank = rank + here.astype(jnp.int32)
    return slots


def gather_kernel(wanted, ciphers, key_count, requests, owner, digits, *refs):
    outs, sems = refs[: len(wanted)], refs[len(wanted)]
    chosen = slot_ciphers(requests, ciphers, key_count, owner[0])
    loads = []
    for out, (slot, block) in zip(outs, wanted):
        for part in range(out.shape[0]):
            source = digits.at[chosen[slot], part, pl.ds(block * ROWS, ROWS)]
            loads.append(pltpu.make_async_copy(source, out.at[part], sems.at[len(loads)]))
    for load in loads:
        load.start()
    for load in loads:
        load.wait()


def gather(digits, requests, owner, wanted):
    ciphers, parts, _, columns = digits.shape
    key_count = requests.shape[1] // lax.axis_size("grp")
    return pl.pallas_call(
        functools.partial(gather_kernel, wanted, ciphers, key_count),
        out_shape=[jax.ShapeDtypeStruct((parts, ROWS, columns), jnp.float32)] * len(wanted),
        in_specs=[SMEM, SMEM, pl.BlockSpec(memory_space=pltpu.HBM)],
        out_specs=[VMEM] * len(wanted),
        scratch_shapes=[pltpu.SemaphoreType.DMA((parts * len(wanted),))],
        compiler_params=pltpu.CompilerParams(vmem_limit_bytes=4 << 20),
        cost_estimate=pl.CostEstimate(
            flops=0, transcendentals=0, bytes_accessed=8 * len(wanted) * parts * ROWS * columns
        ),
        name="gather_digits",
    )(requests, owner, pltpu.with_memory_space_constraint(digits, pltpu.HBM))


def products_kernel(slots, blocks, local, requests, owner, rotations, digits, keys, modulus_ref, tail, resident, rolled):
    key_count, parts, polys, _, columns = keys.shape
    ciphers = requests.shape[0]
    pad = WIDEST // LANES
    tiles = columns // LANES
    tail[...] = jnp.zeros_like(tail)
    resident[...] = jnp.zeros_like(resident)
    rolled[...] = jnp.zeros_like(rolled)
    lane = lax.broadcasted_iota(jnp.int32, (ROWS, LANES), 1)
    chosen = slot_ciphers(requests, ciphers, key_count, owner[0])

    def add_key(step, carry):
        block = step // key_count
        key = step - block * key_count
        rows = pl.ds(pl.multiple_of(block * ROWS, ROWS), ROWS)
        limbs = pl.ds(pl.multiple_of((blocks[0] + block) * ROWS, ROWS), ROWS)
        amount = 2 * rotations[owner[0] * key_count + key]
        skipped = amount // LANES
        within = amount - skipped * LANES
        turn = lax.rem(LANES - within, LANES)
        from_this = lane < LANES - within
        modulus = modulus_ref[limbs, :]
        inverse = 1.0 / modulus
        for place, slot in enumerate(slots):
            source = chosen[slot] if local else place

            @pl.when(requests[chosen[slot], owner[0] * key_count + key] > 0)
            def _():
                for poly in range(polys):
                    for tile in range(tiles):
                        at = pl.ds(tile * LANES, LANES)
                        combined = digits[source, 0, rows, at] * keys[key, 0, poly, limbs, at]
                        for part in range(1, parts):
                            combined = combined + digits[source, part, rows, at] * keys[key, part, poly, limbs, at]
                        quotient = jnp.floor(combined * inverse)
                        remainder = combined - quotient * modulus
                        rolled[:, pl.ds((pad + tile) * LANES, LANES)] = pltpu.roll(remainder, turn, 1)
                    for tile in range(pad + tiles):
                        start = pl.multiple_of((skipped + tile) * LANES, LANES)
                        after = pl.multiple_of((skipped + tile + 1) * LANES, LANES)
                        moved = jnp.where(from_this, rolled[:, pl.ds(start, LANES)], rolled[:, pl.ds(after, LANES)])
                        if tile < pad:
                            at = pl.ds(tile * LANES, LANES)
                            tail[place, poly, rows, at] = tail[place, poly, rows, at] + moved
                        else:
                            at = pl.ds((tile - pad) * LANES, LANES)
                            resident[place, poly, rows, at] = resident[place, poly, rows, at] + moved
        return carry

    lax.fori_loop(0, len(blocks) * key_count, add_key, 0)


def products(digits, keys, requests, owner, rotations, modulus, slots, blocks, local):
    key_count, parts, polys, _, columns = keys.shape
    count = len(slots)
    limbs = len(blocks) * ROWS
    pad = WIDEST // LANES
    work = count * key_count * polys * limbs * columns
    return pl.pallas_call(
        functools.partial(products_kernel, slots, blocks, local),
        out_shape=[
            jax.ShapeDtypeStruct((count, polys, limbs, WIDEST), jnp.float32),
            jax.ShapeDtypeStruct((count, polys, limbs, columns), jnp.float32),
        ],
        in_specs=[SMEM, SMEM, SMEM, VMEM, VMEM, VMEM],
        out_specs=[VMEM, VMEM],
        scratch_shapes=[pltpu.VMEM((ROWS, columns + 2 * pad * LANES + LANES), jnp.float32)],
        compiler_params=pltpu.CompilerParams(vmem_limit_bytes=20 << 20),
        cost_estimate=pl.CostEstimate(
            flops=20 * work, transcendentals=0, bytes_accessed=4 * (key_count * parts * polys * limbs * columns + count * limbs * columns * (parts + polys))
        ),
        name="products",
    )(requests, owner, rotations, digits, keys, modulus)


def add_tail_kernel(arrived, held, out):
    columns = held.shape[-1]
    at = pl.ds(columns - WIDEST, WIDEST)
    out[:, :, :, at] = held[:, :, :, at] + arrived[...]


def add_tail(resident, arrived):
    return pl.pallas_call(
        add_tail_kernel,
        out_shape=jax.ShapeDtypeStruct(resident.shape, jnp.float32),
        in_specs=[VMEM, VMEM],
        out_specs=VMEM,
        input_output_aliases={1: 0},
        compiler_params=pltpu.CompilerParams(vmem_limit_bytes=8 << 20),
        name="add_tail",
    )(arrived, resident)


def reduce_mod(amount, modulus):
    quotient = jnp.floor(amount * (1.0 / modulus))
    remainder = amount - quotient * modulus
    remainder = jnp.where(remainder < 0, remainder + modulus, remainder)
    return jnp.where(remainder >= modulus, remainder - modulus, remainder)


def sums_kernel(owners, groups, ciphers, key_count, keep, requests, me, modulus, *refs):
    parts = refs[: len(owners)]
    out = refs[len(owners)]
    cipher = pl.program_id(1)
    out[...] = jnp.zeros_like(out)
    for part, (steps, slots) in zip(parts, owners):
        chosen = slot_ciphers(requests, ciphers, key_count, lax.rem(me[0] + steps, groups))
        for place, slot in enumerate(slots):

            @pl.when(chosen[slot] == cipher)
            def _():
                out[...] = out[...] + part[place]

    if keep:
        held = refs[len(owners) + 1]
        chosen = slot_ciphers(requests, ciphers, key_count, lax.rem(me[0] + groups - 1, groups))
        for slot in range(CAP):

            @pl.when(chosen[slot] == cipher)
            def _():
                held[slot] = out[...]

    wide = modulus[:, :1]
    out[...] = reduce_mod(out[...], wide) / wide


def sums(parts, owners, requests, me, modulus, ciphers, keep):
    polys, limbs, columns = parts[0].shape[1:]
    groups = lax.axis_size("grp")
    key_count = requests.shape[1] // groups
    shapes = [jax.ShapeDtypeStruct((ciphers, polys, limbs, columns), jnp.float32)]
    specs = [pl.BlockSpec((pl.Squeezed(), polys, ROWS, columns), lambda block, cipher, *_: (cipher, 0, block, 0))]
    if keep:
        shapes.append(jax.ShapeDtypeStruct((CAP, polys, limbs, columns), jnp.float32))
        specs.append(pl.BlockSpec((CAP, polys, ROWS, columns), lambda block, cipher, *_: (0, 0, block, 0)))
    return pl.pallas_call(
        functools.partial(sums_kernel, owners, groups, ciphers, key_count, keep),
        out_shape=shapes,
        grid_spec=pltpu.PrefetchScalarGridSpec(
            num_scalar_prefetch=2,
            grid=(limbs // ROWS, ciphers),
            in_specs=[pl.BlockSpec((ROWS, LANES), lambda block, cipher, *_: (block, 0))]
            + [
                pl.BlockSpec((part.shape[0], polys, ROWS, columns), lambda block, cipher, *_: (0, 0, block, 0))
                for part in parts
            ],
            out_specs=specs,
        ),
        compiler_params=pltpu.CompilerParams(
            dimension_semantics=("arbitrary", "arbitrary"), vmem_limit_bytes=24 << 20
        ),
        cost_estimate=pl.CostEstimate(
            flops=20 * ciphers * polys * limbs * columns,
            transcendentals=0,
            bytes_accessed=4 * (ciphers + 2 + 2 * len(parts)) * polys * limbs * columns,
        ),
        name="sums",
    )(requests, me, modulus, *parts)


def finish_kernel(slot, block, groups, key_count, requests, me, modulus, part, held, before, out, done, sems):
    ciphers, polys, _, _ = out.shape
    cipher = slot_ciphers(requests, ciphers, key_count, lax.rem(me[0] + groups - 1, groups))[slot]
    rows = pl.ds(block * ROWS, ROWS)
    wide = modulus[rows, :1]
    stores = []
    for poly in range(polys):
        done[poly] = reduce_mod(held[slot, poly, rows, :] + part[0, poly], wide) / wide
        stores.append(pltpu.make_async_copy(done.at[poly], out.at[cipher, poly, rows], sems.at[poly]))
        stores[-1].start()
    for store in stores:
        store.wait()


def finish(part, held, result, requests, me, modulus, slot, block):
    _, polys, _, columns = result.shape
    groups = lax.axis_size("grp")
    key_count = requests.shape[1] // groups
    hbm = pl.BlockSpec(memory_space=pltpu.HBM)
    return pl.pallas_call(
        functools.partial(finish_kernel, slot, block, groups, key_count),
        out_shape=jax.ShapeDtypeStruct(result.shape, jnp.float32),
        in_specs=[SMEM, SMEM, VMEM, VMEM, VMEM, hbm],
        out_specs=hbm,
        scratch_shapes=[pltpu.VMEM((polys, ROWS, columns), jnp.float32), pltpu.SemaphoreType.DMA((polys,))],
        input_output_aliases={5: 0},
        compiler_params=pltpu.CompilerParams(vmem_limit_bytes=8 << 20),
        cost_estimate=pl.CostEstimate(
            flops=20 * polys * ROWS * columns, transcendentals=0, bytes_accessed=12 * polys * ROWS * columns
        ),
        name="finish",
    )(requests, me, modulus, part, held, result)


def per_device(digits, keys, requests, rotations, moduli):
    me = lax.axis_index("grp").astype(jnp.int32).reshape(1)
    modulus = jnp.broadcast_to(moduli.astype(jnp.float32)[:, None], (digits.shape[2], LANES))
    way = key_switch_pair if lax.axis_size("grp") == 2 else key_switch_any
    return way(digits, keys, requests, rotations, modulus, me)


def key_switch_any(digits, keys, requests, rotations, modulus, me):
    groups = lax.axis_size("grp")
    blocks = tuple(range(digits.shape[2] // ROWS))
    slots = tuple(range(CAP))
    tail, resident = products(digits, keys, requests, me, rotations, modulus, slots, blocks, True)
    parts = [add_tail(resident, shifted(tail, "limb", -1))]
    owners = [(0, slots)]
    for steps in range(1, groups):
        asked = shifted(requests, "grp", steps)
        owner = lax.rem(me + steps, groups)
        for slot in slots:
            picked = gather(digits, requests, owner, tuple((slot, block) for block in blocks))
            back = []
            for block in blocks:
                arrived = shifted(picked[block], "grp", steps)
                tail, resident = products(
                    arrived[None], keys, asked, me, rotations, modulus, (slot,), (block,), False
                )
                back.append(shifted(add_tail(resident, shifted(tail, "limb", -1)), "grp", -steps))
            parts.append(jnp.concatenate(back, axis=2))
            owners.append((steps, (slot,)))
    return sums(parts, tuple(owners), requests, me, modulus, digits.shape[0], False)[0]


def key_switch_pair(digits, keys, requests, rotations, modulus, me):
    key_count = keys.shape[0]
    other = 1 - me
    asked = shifted(requests, "grp", 1)
    first = gather(digits, requests, other, ((0, 0),))[0]
    ours = jnp.where(me == 0, requests, asked)[:, key_count:]
    theirs = jnp.where(me == 0, asked, requests)[:, :key_count]
    two_right = jnp.sum(jnp.max(ours, axis=1)) > 1
    two_left = jnp.sum(jnp.max(theirs, axis=1)) > 1
    case = jnp.where(two_right == two_left, 0, jnp.where(two_right, 1, 2))

    def branch(pairs):
        def run(first, digits, keys, requests, asked, rotations, modulus, me):
            return exchange(pairs, first, digits, keys, requests, asked, rotations, modulus, me)

        return run

    ways = ([(0, 1), (1, 0)], [(0, 1)], [(1, 0)])
    branches = [branch((ways[0], pairs)) for pairs in ways]
    return lax.switch(case, branches, first, digits, keys, requests, asked, rotations, modulus, me)


def exchange(pairs, first, digits, keys, requests, asked, rotations, modulus, me):
    blocks = tuple(range(digits.shape[2] // ROWS))
    slots = tuple(range(CAP))
    turns = [(slot, block) for slot in slots for block in blocks]
    other = 1 - me
    picked = dict(zip(turns[1:], gather(digits, requests, other, tuple(turns[1:]))))
    picked[turns[0]] = first
    sent = {}
    for slot, block in turns:
        sent[slot, block] = lax.ppermute(picked[slot, block], "grp", pairs[slot])
    tail, resident = products(digits, keys, requests, me, rotations, modulus, slots, blocks, True)
    arrived = shifted(tail, "limb", -1)
    local = add_tail(resident, arrived)
    result, held = sums([local], ((0, slots),), requests, me, modulus, digits.shape[0], True)
    back = {}
    for slot, block in turns:
        tail, resident = products(
            sent[slot, block][None], keys, asked, me, rotations, modulus, (slot,), (block,), False
        )
        arrived = shifted(tail, "limb", -1)
        whole = add_tail(resident, arrived)
        back[slot, block] = lax.ppermute(whole, "grp", [(target, source) for source, target in pairs[slot]])
    for slot, block in turns:
        result = finish(back[slot, block], held, result, requests, me, modulus, slot, block)
    return result


def solution(mesh):
    in_specs = (
        P("grp", None, None, "limb"),
        P("grp", None, None, None, "limb"),
        P("grp", None),
        P(),
        P(),
    )
    out_specs = P("grp", None, None, "limb")
    return jax.shard_map(
        per_device, mesh=mesh, in_specs=in_specs, out_specs=out_specs, check_vma=False
    )
```

```python
import functools

import jax
import jax.numpy as jnp
from jax import lax
from jax.experimental import pallas as pl
from jax.experimental.pallas import tpu as pltpu
from jax.sharding import PartitionSpec as P

RMAX = 256
CAP = 2
WIDEST = 2 * RMAX
LANES = 128
ROWS = 8
SMEM = pl.BlockSpec(memory_space=pltpu.SMEM)
VMEM = pl.BlockSpec(memory_space=pltpu.VMEM)


def shifted(value, axis, steps):
    count = lax.axis_size(axis)
    pairs = [(source, (source + steps) % count) for source in range(count)]
    return lax.ppermute(value, axis, pairs)


def slot_ciphers(requests, ciphers, key_count, owner):
    needed = []
    for cipher in range(ciphers):
        flag = requests[cipher, owner * key_count]
        for key in range(1, key_count):
            flag = flag | requests[cipher, owner * key_count + key]
        needed.append(flag)
    return ranked(needed)


def ranked(needed):
    slots = [jnp.int32(0)] * CAP
    rank = jnp.int32(0)
    for want in (1, 0):
        for cipher in range(len(needed)):
            here = needed[cipher] == want
            for slot in range(CAP):
                slots[slot] = jnp.where(here & (rank == slot), cipher, slots[slot])
            rank = rank + here.astype(jnp.int32)
    return slots


def group_after(steps, groups):
    return lax.rem(lax.axis_index("grp") + steps, groups)


def gather_kernel(wanted, cuts, steps, groups, requests, digits, *refs):
    outs, sems = refs[: len(wanted)], refs[len(wanted)]
    ciphers, parts, _, columns = digits.shape
    chosen = slot_ciphers(requests, ciphers, requests.shape[1] // groups, group_after(steps, groups))
    width = columns // cuts
    loads = []
    for out, (slot, block) in zip(outs, wanted):
        for part in range(parts):
            for cut in range(cuts):
                at = pl.ds(cut * width, width)
                source = digits.at[chosen[slot], part, pl.ds(block * ROWS, ROWS), at]
                loads.append(pltpu.make_async_copy(source, out.at[part, :, at], sems.at[len(loads)]))
    for load in loads:
        load.start()
    for load in loads:
        load.wait()


def gather(digits, requests, steps, wanted, cuts=1):
    parts, _, columns = digits.shape[1:]
    return pl.pallas_call(
        functools.partial(gather_kernel, wanted, cuts, steps, lax.axis_size("grp")),
        out_shape=[jax.ShapeDtypeStruct((parts, ROWS, columns), jnp.float32)] * len(wanted),
        in_specs=[SMEM, pl.BlockSpec(memory_space=pltpu.HBM)],
        out_specs=[VMEM] * len(wanted),
        scratch_shapes=[pltpu.SemaphoreType.DMA((cuts * parts * len(wanted),))],
        compiler_params=pltpu.CompilerParams(vmem_limit_bytes=4 << 20),
        cost_estimate=pl.CostEstimate(
            flops=0, transcendentals=0, bytes_accessed=8 * len(wanted) * parts * ROWS * columns
        ),
        name="gather_digits",
    )(requests, pltpu.with_memory_space_constraint(digits, pltpu.HBM))


def products_kernel(slots, blocks, local, requests, rotations, digits, keys, modulus_ref, tail, resident, rolled):
    key_count, parts, polys, _, columns = keys.shape
    ciphers = requests.shape[0]
    pad = WIDEST // LANES
    tiles = columns // LANES
    tail[...] = jnp.zeros_like(tail)
    resident[...] = jnp.zeros_like(resident)
    rolled[...] = jnp.zeros_like(rolled)
    lane = lax.broadcasted_iota(jnp.int32, (ROWS, LANES), 1)
    me = lax.axis_index("grp")
    chosen = slot_ciphers(requests, ciphers, key_count, me)

    def add_key(step, carry):
        block = step // key_count
        key = step - block * key_count
        rows = pl.ds(pl.multiple_of(block * ROWS, ROWS), ROWS)
        limbs = pl.ds(pl.multiple_of((blocks[0] + block) * ROWS, ROWS), ROWS)
        amount = 2 * rotations[me * key_count + key]
        skipped = amount // LANES
        within = amount - skipped * LANES
        turn = lax.rem(LANES - within, LANES)
        from_this = lane < LANES - within
        modulus = modulus_ref[limbs, :]
        inverse = 1.0 / modulus
        for place, slot in enumerate(slots):
            source = chosen[slot] if local else place

            @pl.when(requests[chosen[slot], me * key_count + key] > 0)
            def _():
                for poly in range(polys):
                    for tile in range(tiles):
                        at = pl.ds(tile * LANES, LANES)
                        combined = digits[source, 0, rows, at] * keys[key, 0, poly, limbs, at]
                        for part in range(1, parts):
                            combined = combined + digits[source, part, rows, at] * keys[key, part, poly, limbs, at]
                        quotient = jnp.floor(combined * inverse)
                        remainder = combined - quotient * modulus
                        rolled[:, pl.ds((pad + tile) * LANES, LANES)] = pltpu.roll(remainder, turn, 1)
                    for tile in range(pad + tiles):
                        start = pl.multiple_of((skipped + tile) * LANES, LANES)
                        after = pl.multiple_of((skipped + tile + 1) * LANES, LANES)
                        moved = jnp.where(from_this, rolled[:, pl.ds(start, LANES)], rolled[:, pl.ds(after, LANES)])
                        if tile < pad:
                            at = pl.ds(tile * LANES, LANES)
                            tail[place, poly, rows, at] = tail[place, poly, rows, at] + moved
                        else:
                            at = pl.ds((tile - pad) * LANES, LANES)
                            resident[place, poly, rows, at] = resident[place, poly, rows, at] + moved
        return carry

    lax.fori_loop(0, len(blocks) * key_count, add_key, 0)


def products(digits, keys, requests, rotations, modulus, slots, blocks, local):
    key_count, parts, polys, _, columns = keys.shape
    count = len(slots)
    limbs = len(blocks) * ROWS
    pad = WIDEST // LANES
    work = count * key_count * polys * limbs * columns
    return pl.pallas_call(
        functools.partial(products_kernel, slots, blocks, local),
        out_shape=[
            jax.ShapeDtypeStruct((count, polys, limbs, WIDEST), jnp.float32),
            jax.ShapeDtypeStruct((count, polys, limbs, columns), jnp.float32),
        ],
        in_specs=[SMEM, SMEM, VMEM, VMEM, VMEM],
        out_specs=[VMEM, VMEM],
        scratch_shapes=[pltpu.VMEM((ROWS, columns + 2 * pad * LANES + LANES), jnp.float32)],
        compiler_params=pltpu.CompilerParams(vmem_limit_bytes=20 << 20),
        cost_estimate=pl.CostEstimate(
            flops=20 * work, transcendentals=0, bytes_accessed=4 * (key_count * parts * polys * limbs * columns + count * limbs * columns * (parts + polys))
        ),
        name="products",
    )(requests, rotations, digits, keys, modulus)


def add_tail_kernel(arrived, held, out):
    columns = held.shape[-1]
    at = pl.ds(columns - WIDEST, WIDEST)
    out[:, :, :, at] = held[:, :, :, at] + arrived[...]


def add_tail(resident, arrived):
    return pl.pallas_call(
        add_tail_kernel,
        out_shape=jax.ShapeDtypeStruct(resident.shape, jnp.float32),
        in_specs=[VMEM, VMEM],
        out_specs=VMEM,
        input_output_aliases={1: 0},
        compiler_params=pltpu.CompilerParams(vmem_limit_bytes=8 << 20),
        name="add_tail",
    )(arrived, resident)


def reduce_mod(amount, modulus):
    quotient = jnp.floor(amount * (1.0 / modulus))
    remainder = amount - quotient * modulus
    remainder = jnp.where(remainder < 0, remainder + modulus, remainder)
    return jnp.where(remainder >= modulus, remainder - modulus, remainder)


def sums_kernel(owners, groups, ciphers, key_count, keep, requests, modulus, *refs):
    parts = refs[: len(owners)]
    out = refs[len(owners)]
    cipher = pl.program_id(1)
    out[...] = jnp.zeros_like(out)
    for part, (steps, slots) in zip(parts, owners):
        chosen = slot_ciphers(requests, ciphers, key_count, group_after(steps, groups))
        for place, slot in enumerate(slots):

            @pl.when(chosen[slot] == cipher)
            def _():
                out[...] = out[...] + part[place]

    if keep:
        held = refs[len(owners) + 1]
        chosen = slot_ciphers(requests, ciphers, key_count, group_after(groups - 1, groups))
        for slot in range(CAP):

            @pl.when(chosen[slot] == cipher)
            def _():
                held[slot] = out[...]

    wide = modulus[:, :1]
    out[...] = reduce_mod(out[...], wide) / wide


def sums(parts, owners, requests, modulus, ciphers, keep):
    polys, limbs, columns = parts[0].shape[1:]
    groups = lax.axis_size("grp")
    key_count = requests.shape[1] // groups
    shapes = [jax.ShapeDtypeStruct((ciphers, polys, limbs, columns), jnp.float32)]
    specs = [pl.BlockSpec((pl.Squeezed(), polys, ROWS, columns), lambda block, cipher, *_: (cipher, 0, block, 0))]
    if keep:
        shapes.append(jax.ShapeDtypeStruct((CAP, polys, limbs, columns), jnp.float32))
        specs.append(pl.BlockSpec((CAP, polys, ROWS, columns), lambda block, cipher, *_: (0, 0, block, 0)))
    return pl.pallas_call(
        functools.partial(sums_kernel, owners, groups, ciphers, key_count, keep),
        out_shape=shapes,
        grid_spec=pltpu.PrefetchScalarGridSpec(
            num_scalar_prefetch=1,
            grid=(limbs // ROWS, ciphers),
            in_specs=[pl.BlockSpec((ROWS, LANES), lambda block, cipher, *_: (block, 0))]
            + [
                pl.BlockSpec((part.shape[0], polys, ROWS, columns), lambda block, cipher, *_: (0, 0, block, 0))
                for part in parts
            ],
            out_specs=specs,
        ),
        compiler_params=pltpu.CompilerParams(
            dimension_semantics=("arbitrary", "arbitrary"), vmem_limit_bytes=24 << 20
        ),
        cost_estimate=pl.CostEstimate(
            flops=20 * ciphers * polys * limbs * columns,
            transcendentals=0,
            bytes_accessed=4 * (ciphers + 2 + 2 * len(parts)) * polys * limbs * columns,
        ),
        name="sums",
    )(requests, modulus, *parts)


def finish_kernel(slot, block, groups, requests, modulus, part, held, before, out, done, sems):
    ciphers, polys, _, _ = out.shape
    key_count = requests.shape[1] // groups
    rows = pl.ds(block * ROWS, ROWS)
    wide = modulus[rows, :1]
    for poly in range(polys):
        done[poly] = reduce_mod(held[slot, poly, rows, :] + part[0, poly], wide) / wide
    asks = requests[...]
    column = lax.broadcasted_iota(jnp.int32, asks.shape, 1) // key_count
    row = lax.broadcasted_iota(jnp.int32, asks.shape, 0)
    asks = jnp.where(column == group_after(groups - 1, groups), asks, 0)
    needed = [jnp.max(jnp.where(row == cipher, asks, 0)) for cipher in range(ciphers)]
    cipher = ranked(needed)[slot]
    stores = [
        pltpu.make_async_copy(done.at[poly], out.at[cipher, poly, rows], sems.at[poly]) for poly in range(polys)
    ]
    for store in stores:
        store.start()
    for store in stores:
        store.wait()


def finish(part, held, result, requests, modulus, slot, block):
    _, polys, _, columns = result.shape
    groups = lax.axis_size("grp")
    hbm = pl.BlockSpec(memory_space=pltpu.HBM)
    return pl.pallas_call(
        functools.partial(finish_kernel, slot, block, groups),
        out_shape=jax.ShapeDtypeStruct(result.shape, jnp.float32),
        in_specs=[VMEM, VMEM, VMEM, VMEM, hbm],
        out_specs=hbm,
        scratch_shapes=[pltpu.VMEM((polys, ROWS, columns), jnp.float32), pltpu.SemaphoreType.DMA((polys,))],
        input_output_aliases={4: 0},
        compiler_params=pltpu.CompilerParams(vmem_limit_bytes=8 << 20),
        cost_estimate=pl.CostEstimate(
            flops=20 * polys * ROWS * columns, transcendentals=0, bytes_accessed=12 * polys * ROWS * columns
        ),
        name="finish",
    )(requests, modulus, part, held, result)


def per_device(digits, keys, requests, rotations, moduli):
    modulus = jnp.broadcast_to(moduli.astype(jnp.float32)[:, None], (digits.shape[2], LANES))
    way = key_switch_pair if lax.axis_size("grp") == 2 else key_switch_any
    return way(digits, keys, requests, rotations, modulus)


def key_switch_any(digits, keys, requests, rotations, modulus):
    groups = lax.axis_size("grp")
    blocks = tuple(range(digits.shape[2] // ROWS))
    slots = tuple(range(CAP))
    tail, resident = products(digits, keys, requests, rotations, modulus, slots, blocks, True)
    parts = [add_tail(resident, shifted(tail, "limb", -1))]
    owners = [(0, slots)]
    for steps in range(1, groups):
        asked = shifted(requests, "grp", steps)
        for slot in slots:
            picked = gather(digits, requests, steps, tuple((slot, block) for block in blocks))
            back = []
            for block in blocks:
                arrived = shifted(picked[block], "grp", steps)
                tail, resident = products(
                    arrived[None], keys, asked, rotations, modulus, (slot,), (block,), False
                )
                back.append(shifted(add_tail(resident, shifted(tail, "limb", -1)), "grp", -steps))
            parts.append(jnp.concatenate(back, axis=2))
            owners.append((steps, (slot,)))
    return sums(parts, tuple(owners), requests, modulus, digits.shape[0], False)[0]


def key_switch_pair(digits, keys, requests, rotations, modulus):
    blocks = tuple(range(digits.shape[2] // ROWS))
    slots = tuple(range(CAP))
    key_count = keys.shape[0]
    both = [(0, 1), (1, 0)]
    turns = [(slot, block) for slot in slots for block in blocks]
    picked = {turns[0]: gather(digits, requests, 1, (turns[0],), 4)[0]}
    picked.update(zip(turns[1:], gather(digits, requests, 1, tuple(turns[1:]))))
    sent = {}
    for block in blocks:
        sent[0, block] = lax.ppermute(picked[0, block], "grp", both)
    asked = shifted(requests, "grp", 1)
    tail, resident = products(digits, keys, requests, rotations, modulus, slots, blocks, True)
    arrived = shifted(tail, "limb", -1)
    local = add_tail(resident, arrived)
    me = lax.axis_index("grp")
    rightward = jnp.where(me == 0, requests, asked)[:, key_count:]
    leftward = jnp.where(me == 0, asked, requests)[:, :key_count]
    two_right = jnp.sum(jnp.max(rightward, axis=1)) > 1
    two_left = jnp.sum(jnp.max(leftward, axis=1)) > 1
    case = jnp.where(two_right == two_left, 0, jnp.where(two_right, 1, 2))
    ahead = remote(sent[0, 0], keys, asked, rotations, modulus, 0, 0)

    def branch(pairs):
        def run(*operands):
            return exchange((both, pairs), *operands)

        return run

    branches = [branch(pairs) for pairs in (both, [(0, 1)], [(1, 0)])]
    operands = (ahead, [picked[turn] for turn in turns[len(blocks) :]], [sent[0, block] for block in blocks[1:]], local)
    return lax.switch(case, branches, *operands, keys, requests, asked, rotations, modulus)


def remote(arrived, keys, asked, rotations, modulus, slot, block):
    tail, resident = products(arrived[None], keys, asked, rotations, modulus, (slot,), (block,), False)
    wrapped = shifted(tail, "limb", -1)
    return add_tail(resident, wrapped)


def exchange(pairs, ahead, picked, arrived, local, keys, requests, asked, rotations, modulus):
    ciphers = requests.shape[0]
    blocks = local.shape[2] // ROWS
    turns = [(slot, block) for slot in range(CAP) for block in range(blocks)]
    sent = dict(zip(turns[1:blocks], arrived))
    for (slot, block), piece in zip(turns[blocks:], picked):
        sent[slot, block] = lax.ppermute(piece, "grp", pairs[slot])
    result, held = sums([local], ((0, tuple(range(CAP))),), requests, modulus, ciphers, True)
    back = {}
    for turn in turns:
        slot, block = turn
        whole = ahead if turn == turns[0] else remote(sent[turn], keys, asked, rotations, modulus, slot, block)
        back[turn] = lax.ppermute(whole, "grp", [(target, source) for source, target in pairs[slot]])
    for slot, block in turns:
        result = finish(back[slot, block], held, result, requests, modulus, slot, block)
    return result


def solution(mesh):
    in_specs = (
        P("grp", None, None, "limb"),
        P("grp", None, None, None, "limb"),
        P("grp", None),
        P(),
        P(),
    )
    out_specs = P("grp", None, None, "limb")
    return jax.shard_map(
        per_device, mesh=mesh, in_specs=in_specs, out_specs=out_specs, check_vma=False
    )
```

```python
import functools

import jax
import jax.numpy as jnp
from jax import lax
from jax.experimental import pallas as pl
from jax.experimental.pallas import tpu as pltpu
from jax.sharding import PartitionSpec as P

RMAX = 256
CAP = 2
WIDEST = 2 * RMAX
LANES = 128
ROWS = 8
SMEM = pl.BlockSpec(memory_space=pltpu.SMEM)
VMEM = pl.BlockSpec(memory_space=pltpu.VMEM)


def shifted(value, axis, steps):
    count = lax.axis_size(axis)
    pairs = [(source, (source + steps) % count) for source in range(count)]
    return lax.ppermute(value, axis, pairs)


def slot_ciphers(requests, ciphers, key_count, owner):
    needed = []
    for cipher in range(ciphers):
        flag = requests[cipher, owner * key_count]
        for key in range(1, key_count):
            flag = flag | requests[cipher, owner * key_count + key]
        needed.append(flag)
    return ranked(needed)


def ranked(needed):
    slots = [jnp.int32(0)] * len(needed)
    rank = jnp.int32(0)
    for want in (1, 0):
        for cipher in range(len(needed)):
            here = needed[cipher] == want
            for slot in range(len(needed)):
                slots[slot] = jnp.where(here & (rank == slot), cipher, slots[slot])
            rank = rank + here.astype(jnp.int32)
    return slots


def group_after(steps, groups):
    return lax.rem(lax.axis_index("grp") + steps, groups)


def gather_kernel(wanted, cuts, steps, groups, requests, digits, *refs):
    outs, sems = refs[: len(wanted)], refs[len(wanted)]
    ciphers, parts, _, columns = digits.shape
    chosen = slot_ciphers(requests, ciphers, requests.shape[1] // groups, group_after(steps, groups))
    width = columns // cuts
    loads = []
    for out, (slot, block) in zip(outs, wanted):
        for part in range(parts):
            for cut in range(cuts):
                at = pl.ds(cut * width, width)
                source = digits.at[chosen[slot], part, pl.ds(block * ROWS, ROWS), at]
                loads.append(pltpu.make_async_copy(source, out.at[part, :, at], sems.at[len(loads)]))
    for load in loads:
        load.start()
    for load in loads:
        load.wait()


def gather(digits, requests, steps, wanted, cuts=1):
    parts, _, columns = digits.shape[1:]
    return pl.pallas_call(
        functools.partial(gather_kernel, wanted, cuts, steps, lax.axis_size("grp")),
        out_shape=[jax.ShapeDtypeStruct((parts, ROWS, columns), jnp.float32)] * len(wanted),
        in_specs=[SMEM, pl.BlockSpec(memory_space=pltpu.HBM)],
        out_specs=[VMEM] * len(wanted),
        scratch_shapes=[pltpu.SemaphoreType.DMA((cuts * parts * len(wanted),))],
        compiler_params=pltpu.CompilerParams(vmem_limit_bytes=4 << 20),
        cost_estimate=pl.CostEstimate(
            flops=0, transcendentals=0, bytes_accessed=8 * len(wanted) * parts * ROWS * columns
        ),
        name="gather_digits",
    )(requests, pltpu.with_memory_space_constraint(digits, pltpu.HBM))


def products_kernel(slots, blocks, local, load, requests, rotations, digits, keys, modulus_ref, tail, resident, *refs):
    key_count, parts, polys, _, columns = keys.shape
    ciphers = requests.shape[0]
    pad = WIDEST // LANES
    tiles = columns // LANES
    rolled = refs[0]
    me = lax.axis_index("grp")
    chosen = slot_ciphers(requests, ciphers, key_count, me)
    first = blocks[0]

    def wanted(key):
        flag = requests[chosen[slots[0]], me * key_count + key]
        for slot in slots[1:]:
            flag = flag | requests[chosen[slot], me * key_count + key]
        return flag > 0

    if load:
        whole, (keys, sems) = keys, refs[1:]
        here = pl.ds(blocks[0] * ROWS, len(blocks) * ROWS)
        first = 0

        def copy(key):
            return pltpu.make_async_copy(whole.at[key, :, :, here], keys.at[key], sems.at[key])

        for key in range(key_count):
            pl.when(wanted(key))(copy(key).start)

    tail[...] = jnp.zeros_like(tail)
    resident[...] = jnp.zeros_like(resident)
    rolled[...] = jnp.zeros_like(rolled)
    lane = lax.broadcasted_iota(jnp.int32, (ROWS, LANES), 1)

    def add_key(key, block):
        rows = pl.ds(pl.multiple_of(block * ROWS, ROWS), ROWS)
        limbs = pl.ds(pl.multiple_of((first + block) * ROWS, ROWS), ROWS)
        amount = 2 * rotations[me * key_count + key]
        skipped = amount // LANES
        within = amount - skipped * LANES
        turn = lax.rem(LANES - within, LANES)
        from_this = lane < LANES - within
        modulus = modulus_ref[pl.ds(pl.multiple_of((blocks[0] + block) * ROWS, ROWS), ROWS), :]
        inverse = 1.0 / modulus
        for place, slot in enumerate(slots):
            source = chosen[slot] if local else place

            @pl.when(requests[chosen[slot], me * key_count + key] > 0)
            def _():
                for poly in range(polys):
                    for tile in range(tiles):
                        at = pl.ds(tile * LANES, LANES)
                        combined = digits[source, 0, rows, at] * keys[key, 0, poly, limbs, at]
                        for part in range(1, parts):
                            combined = combined + digits[source, part, rows, at] * keys[key, part, poly, limbs, at]
                        quotient = jnp.floor(combined * inverse)
                        remainder = combined - quotient * modulus
                        rolled[:, pl.ds((pad + tile) * LANES, LANES)] = pltpu.roll(remainder, turn, 1)
                    for tile in range(pad + tiles):
                        start = pl.multiple_of((skipped + tile) * LANES, LANES)
                        after = pl.multiple_of((skipped + tile + 1) * LANES, LANES)
                        moved = jnp.where(from_this, rolled[:, pl.ds(start, LANES)], rolled[:, pl.ds(after, LANES)])
                        if tile < pad:
                            at = pl.ds(tile * LANES, LANES)
                            tail[place, poly, rows, at] = tail[place, poly, rows, at] + moved
                        else:
                            at = pl.ds((tile - pad) * LANES, LANES)
                            resident[place, poly, rows, at] = resident[place, poly, rows, at] + moved

    def add_step(step, carry):
        key = step // len(blocks)
        block = step - key * len(blocks)
        if load:
            pl.when((block == 0) & wanted(key))(lambda: copy(key).wait())

        add_key(key, block)
        return carry

    lax.fori_loop(0, len(blocks) * key_count, add_step, 0)


def products(digits, keys, requests, rotations, modulus, slots, blocks, local, load):
    key_count, parts, polys, _, columns = keys.shape
    count = len(slots)
    limbs = len(blocks) * ROWS
    pad = WIDEST // LANES
    work = count * key_count * polys * limbs * columns
    scratch = [pltpu.VMEM((ROWS, columns + 2 * pad * LANES + LANES), jnp.float32)]
    if load:
        scratch.append(pltpu.VMEM((key_count, parts, polys, limbs, columns), jnp.float32))
        scratch.append(pltpu.SemaphoreType.DMA((key_count,)))
        keys = pltpu.with_memory_space_constraint(keys, pltpu.HBM)
    return pl.pallas_call(
        functools.partial(products_kernel, slots, blocks, local, load),
        out_shape=[
            jax.ShapeDtypeStruct((count, polys, limbs, WIDEST), jnp.float32),
            jax.ShapeDtypeStruct((count, polys, limbs, columns), jnp.float32),
        ],
        in_specs=[SMEM, SMEM, VMEM, pl.BlockSpec(memory_space=pltpu.HBM) if load else VMEM, VMEM],
        out_specs=[VMEM, VMEM],
        scratch_shapes=scratch,
        compiler_params=pltpu.CompilerParams(vmem_limit_bytes=20 << 20),
        cost_estimate=pl.CostEstimate(
            flops=20 * work,
            transcendentals=0,
            bytes_accessed=4 * (key_count * parts * polys * limbs * columns + count * limbs * columns * (parts + polys)),
        ),
        name="products",
    )(requests, rotations, digits, keys, modulus)


def add_tail_kernel(arrived, held, out):
    columns = held.shape[-1]
    at = pl.ds(columns - WIDEST, WIDEST)
    out[:, :, :, at] = held[:, :, :, at] + arrived[...]


def add_tail(resident, arrived):
    return pl.pallas_call(
        add_tail_kernel,
        out_shape=jax.ShapeDtypeStruct(resident.shape, jnp.float32),
        in_specs=[VMEM, VMEM],
        out_specs=VMEM,
        input_output_aliases={1: 0},
        compiler_params=pltpu.CompilerParams(vmem_limit_bytes=8 << 20),
        name="add_tail",
    )(arrived, resident)


def reduce_mod(amount, modulus):
    quotient = jnp.floor(amount * (1.0 / modulus))
    remainder = amount - quotient * modulus
    remainder = jnp.where(remainder < 0, remainder + modulus, remainder)
    return jnp.where(remainder >= modulus, remainder - modulus, remainder)


def sums_kernel(owners, groups, ciphers, key_count, requests, modulus, *refs):
    parts, out = refs[: len(owners)], refs[len(owners)]
    cipher = pl.program_id(1)
    out[...] = jnp.zeros_like(out)
    for part, (steps, slots) in zip(parts, owners):
        chosen = slot_ciphers(requests, ciphers, key_count, group_after(steps, groups))
        for place, slot in enumerate(slots):

            @pl.when(chosen[slot] == cipher)
            def _():
                out[...] = out[...] + part[place]

    wide = modulus[:, :1]
    out[...] = reduce_mod(out[...], wide) / wide


def sums(parts, owners, requests, modulus, ciphers):
    polys, limbs, columns = parts[0].shape[1:]
    groups = lax.axis_size("grp")
    key_count = requests.shape[1] // groups
    return pl.pallas_call(
        functools.partial(sums_kernel, owners, groups, ciphers, key_count),
        out_shape=jax.ShapeDtypeStruct((ciphers, polys, limbs, columns), jnp.float32),
        grid_spec=pltpu.PrefetchScalarGridSpec(
            num_scalar_prefetch=1,
            grid=(limbs // ROWS, ciphers),
            in_specs=[pl.BlockSpec((ROWS, LANES), lambda block, cipher, *_: (block, 0))]
            + [
                pl.BlockSpec((part.shape[0], polys, ROWS, columns), lambda block, cipher, *_: (0, 0, block, 0))
                for part in parts
            ],
            out_specs=pl.BlockSpec(
                (pl.Squeezed(), polys, ROWS, columns), lambda block, cipher, *_: (cipher, 0, block, 0)
            ),
        ),
        compiler_params=pltpu.CompilerParams(
            dimension_semantics=("arbitrary", "arbitrary"), vmem_limit_bytes=24 << 20
        ),
        name="sums",
    )(requests, modulus, *parts)


def orders_of(requests, groups):
    ciphers, columns = requests.shape
    key_count = columns // groups
    bits = key_count.bit_length()
    asks = requests[...]
    row = lax.broadcasted_iota(jnp.int32, asks.shape, 0)
    owner = lax.broadcasted_iota(jnp.int32, asks.shape, 1) // key_count
    me = group_after(0, groups)
    after = group_after(1, groups)
    place = jnp.where(owner == me, 0, ciphers) + row
    code = jnp.sum(jnp.where((owner == me) | (owner == after), asks << (place * bits), 0))
    flags = [
        ((code >> (place * bits)) & ((1 << bits) - 1) > 0).astype(jnp.int32) for place in range(2 * ciphers)
    ]
    return ranked(flags[:ciphers]), ranked(flags[ciphers:]), flags[:ciphers]


def finish_kernel(ranks, blocks, groups, requests, modulus, local, *refs):
    part = None
    if len(refs) == 5:
        part, _, out, done, sems = refs
    else:
        out, done, sems = refs
    polys = out.shape[1]
    ours, theirs, _ = orders_of(requests, groups)
    stores = []
    for at, rank in enumerate(ranks):
        cipher = theirs[rank]
        weights = [jnp.where(ours[slot] == cipher, 1.0, 0.0) for slot in range(CAP)]
        for which, block in enumerate(blocks):
            rows = pl.ds(block * ROWS, ROWS)
            here = pl.ds(which * ROWS, ROWS)
            wide = modulus[rows, :1]
            for poly in range(polys):
                total = local[0, poly, rows, :] * weights[0]
                for slot in range(1, CAP):
                    total = total + local[slot, poly, rows, :] * weights[slot]
                if part is not None:
                    total = total + part[0, poly]
                done[at, poly, here, :] = reduce_mod(total, wide) / wide
                stores.append(
                    pltpu.make_async_copy(done.at[at, poly, here], out.at[cipher, poly, rows], sems.at[len(stores)])
                )
                stores[-1].start()
    for store in stores:
        store.wait()


def finish(local, requests, modulus, ciphers, ranks, blocks, part=None, before=None):
    _, polys, _, columns = local.shape
    hbm = pl.BlockSpec(memory_space=pltpu.HBM)
    limbs = modulus.shape[0]
    work = len(ranks) * polys * len(blocks) * ROWS * columns
    more = [] if part is None else [part, before]
    return pl.pallas_call(
        functools.partial(finish_kernel, ranks, blocks, lax.axis_size("grp")),
        out_shape=jax.ShapeDtypeStruct((ciphers, polys, limbs, columns), jnp.float32),
        in_specs=[VMEM, VMEM, VMEM] + ([] if part is None else [VMEM, hbm]),
        out_specs=hbm,
        scratch_shapes=[
            pltpu.VMEM((len(ranks), polys, len(blocks) * ROWS, columns), jnp.float32),
            pltpu.SemaphoreType.DMA((len(ranks) * polys * len(blocks),)),
        ],
        input_output_aliases={} if part is None else {4: 0},
        compiler_params=pltpu.CompilerParams(vmem_limit_bytes=8 << 20),
        cost_estimate=pl.CostEstimate(flops=20 * work, transcendentals=0, bytes_accessed=12 * work),
        name="finish",
    )(requests, modulus, local, *more)


def per_device(digits, keys, requests, rotations, moduli):
    modulus = jnp.broadcast_to(moduli.astype(jnp.float32)[:, None], (digits.shape[2], LANES))
    way = key_switch_pair if lax.axis_size("grp") == 2 else key_switch_any
    return way(digits, keys, requests, rotations, modulus)


def key_switch_any(digits, keys, requests, rotations, modulus):
    groups = lax.axis_size("grp")
    blocks = tuple(range(digits.shape[2] // ROWS))
    slots = tuple(range(CAP))
    tail, resident = products(digits, keys, requests, rotations, modulus, slots, blocks, True, True)
    parts = [add_tail(resident, shifted(tail, "limb", -1))]
    owners = [(0, slots)]
    for steps in range(1, groups):
        asked = shifted(requests, "grp", steps)
        for slot in slots:
            picked = gather(digits, requests, steps, tuple((slot, block) for block in blocks))
            back = []
            for block in blocks:
                arrived = shifted(picked[block], "grp", steps)
                tail, resident = products(
                    arrived[None], keys, asked, rotations, modulus, (slot,), (block,), False, True
                )
                back.append(shifted(add_tail(resident, shifted(tail, "limb", -1)), "grp", -steps))
            parts.append(jnp.concatenate(back, axis=2))
            owners.append((steps, (slot,)))
    return sums(parts, tuple(owners), requests, modulus, digits.shape[0])


def key_switch_pair(digits, keys, requests, rotations, modulus):
    blocks = tuple(range(digits.shape[2] // ROWS))
    slots = tuple(range(CAP))
    key_count = keys.shape[0]
    both = [(0, 1), (1, 0)]
    turns = [(slot, block) for slot in slots for block in blocks]
    picked = {turns[0]: gather(digits, requests, 1, (turns[0],), 4)[0]}
    picked.update(zip(turns[1:], gather(digits, requests, 1, tuple(turns[1:]))))
    sent = {}
    for block in blocks:
        sent[0, block] = lax.ppermute(picked[0, block], "grp", both)
    asked = shifted(requests, "grp", 1)
    tail, resident = products(digits, keys, requests, rotations, modulus, slots, blocks, True, True)
    arrived = shifted(tail, "limb", -1)
    local = add_tail(resident, arrived)
    me = lax.axis_index("grp")
    rightward = jnp.where(me == 0, requests, asked)[:, key_count:]
    leftward = jnp.where(me == 0, asked, requests)[:, :key_count]
    two_right = jnp.sum(jnp.max(rightward, axis=1)) > 1
    two_left = jnp.sum(jnp.max(leftward, axis=1)) > 1
    case = jnp.where(two_right == two_left, 0, jnp.where(two_right, 1, 2))
    ahead = remote(sent[0, 0], keys, asked, rotations, modulus, 0, 0)

    def branch(pairs):
        def run(*operands):
            return exchange((both, pairs), *operands)

        return run

    branches = [branch(pairs) for pairs in (both, [(0, 1)], [(1, 0)])]
    operands = (ahead, [picked[turn] for turn in turns[len(blocks) :]], [sent[0, block] for block in blocks[1:]], local)
    return lax.switch(case, branches, *operands, keys, requests, asked, rotations, modulus)


def remote(arrived, keys, asked, rotations, modulus, slot, block):
    tail, resident = products(arrived[None], keys, asked, rotations, modulus, (slot,), (block,), False, slot == 0)
    wrapped = shifted(tail, "limb", -1)
    return add_tail(resident, wrapped)


def exchange(pairs, ahead, picked, arrived, local, keys, requests, asked, rotations, modulus):
    ciphers = requests.shape[0]
    blocks = local.shape[2] // ROWS
    turns = [(slot, block) for slot in range(CAP) for block in range(blocks)]
    sent = dict(zip(turns[1:blocks], arrived))
    for (slot, block), piece in zip(turns[blocks:], picked):
        sent[slot, block] = lax.ppermute(piece, "grp", pairs[slot])
    result = finish(local, requests, modulus, ciphers, tuple(range(CAP, ciphers)), tuple(range(blocks)))
    back = {}
    for turn in turns:
        slot, block = turn
        whole = ahead if turn == turns[0] else remote(sent[turn], keys, asked, rotations, modulus, slot, block)
        back[turn] = lax.ppermute(whole, "grp", [(target, source) for source, target in pairs[slot]])
    for slot, block in turns:
        result = finish(local, requests, modulus, ciphers, (slot,), (block,), back[slot, block], result)
    return result


def solution(mesh):
    in_specs = (
        P("grp", None, None, "limb"),
        P("grp", None, None, None, "limb"),
        P("grp", None),
        P(),
        P(),
    )
    out_specs = P("grp", None, None, "limb")
    return jax.shard_map(
        per_device, mesh=mesh, in_specs=in_specs, out_specs=out_specs, check_vma=False
    )
```

```python
import functools

import jax
import jax.numpy as jnp
from jax import lax
from jax.experimental import pallas as pl
from jax.experimental.pallas import tpu as pltpu
from jax.sharding import PartitionSpec as P

RMAX = 256
CAP = 2
WIDEST = 2 * RMAX
LANES = 128
ROWS = 8
SMEM = pl.BlockSpec(memory_space=pltpu.SMEM)
VMEM = pl.BlockSpec(memory_space=pltpu.VMEM)


def shifted(value, axis, steps):
    count = lax.axis_size(axis)
    pairs = [(source, (source + steps) % count) for source in range(count)]
    return lax.ppermute(value, axis, pairs)


def slot_ciphers(requests, ciphers, key_count, owner):
    needed = []
    for cipher in range(ciphers):
        flag = requests[cipher, owner * key_count]
        for key in range(1, key_count):
            flag = flag | requests[cipher, owner * key_count + key]
        needed.append(flag)
    return ranked(needed)


def ranked(needed):
    slots = [jnp.int32(0)] * len(needed)
    rank = jnp.int32(0)
    for want in (1, 0):
        for cipher in range(len(needed)):
            here = needed[cipher] == want
            for slot in range(len(needed)):
                slots[slot] = jnp.where(here & (rank == slot), cipher, slots[slot])
            rank = rank + here.astype(jnp.int32)
    return slots


def group_after(steps, groups):
    return lax.rem(lax.axis_index("grp") + steps, groups)


def gather_kernel(wanted, cuts, steps, groups, requests, digits, *refs):
    outs, sems = refs[: len(wanted)], refs[len(wanted)]
    ciphers, parts, _, columns = digits.shape
    chosen = slot_ciphers(requests, ciphers, requests.shape[1] // groups, group_after(steps, groups))
    width = columns // cuts
    loads = []
    for out, (slot, block) in zip(outs, wanted):
        for part in range(parts):
            for cut in range(cuts):
                at = pl.ds(cut * width, width)
                source = digits.at[chosen[slot], part, pl.ds(block * ROWS, ROWS), at]
                loads.append(pltpu.make_async_copy(source, out.at[part, :, at], sems.at[len(loads)]))
    for load in loads:
        load.start()
    for load in loads:
        load.wait()


def gather(digits, requests, steps, wanted, cuts=1):
    parts, _, columns = digits.shape[1:]
    return pl.pallas_call(
        functools.partial(gather_kernel, wanted, cuts, steps, lax.axis_size("grp")),
        out_shape=[jax.ShapeDtypeStruct((parts, ROWS, columns), jnp.float32)] * len(wanted),
        in_specs=[SMEM, pl.BlockSpec(memory_space=pltpu.HBM)],
        out_specs=[VMEM] * len(wanted),
        scratch_shapes=[pltpu.SemaphoreType.DMA((cuts * parts * len(wanted),))],
        compiler_params=pltpu.CompilerParams(vmem_limit_bytes=4 << 20),
        cost_estimate=pl.CostEstimate(
            flops=0, transcendentals=0, bytes_accessed=8 * len(wanted) * parts * ROWS * columns
        ),
        name="gather_digits",
    )(requests, pltpu.with_memory_space_constraint(digits, pltpu.HBM))


def products_kernel(slots, blocks, local, load, requests, rotations, digits, keys, modulus_ref, tail, resident, *refs):
    key_count, parts, polys, _, columns = keys.shape
    ciphers = requests.shape[0]
    pad = WIDEST // LANES
    tiles = columns // LANES
    rolled = refs[0]
    me = lax.axis_index("grp")
    chosen = slot_ciphers(requests, ciphers, key_count, me)
    first = blocks[0]

    def wanted(key):
        flag = requests[chosen[slots[0]], me * key_count + key]
        for slot in slots[1:]:
            flag = flag | requests[chosen[slot], me * key_count + key]
        return flag > 0

    if load:
        whole, (keys, sems) = keys, refs[1:]
        here = pl.ds(blocks[0] * ROWS, len(blocks) * ROWS)
        first = 0

        def copy(key):
            return pltpu.make_async_copy(whole.at[key, :, :, here], keys.at[key], sems.at[key])

        for key in range(key_count):
            pl.when(wanted(key))(copy(key).start)

    tail[...] = jnp.zeros_like(tail)
    resident[...] = jnp.zeros_like(resident)
    rolled[...] = jnp.zeros_like(rolled)
    lane = lax.broadcasted_iota(jnp.int32, (ROWS, LANES), 1)

    def add_key(key, block):
        rows = pl.ds(pl.multiple_of(block * ROWS, ROWS), ROWS)
        limbs = pl.ds(pl.multiple_of((first + block) * ROWS, ROWS), ROWS)
        amount = 2 * rotations[me * key_count + key]
        skipped = amount // LANES
        within = amount - skipped * LANES
        turn = lax.rem(LANES - within, LANES)
        from_this = lane < LANES - within
        modulus = modulus_ref[pl.ds(pl.multiple_of((blocks[0] + block) * ROWS, ROWS), ROWS), :]
        inverse = 1.0 / modulus
        for place, slot in enumerate(slots):
            source = chosen[slot] if local else place

            @pl.when(requests[chosen[slot], me * key_count + key] > 0)
            def _():
                for poly in range(polys):
                    for tile in range(tiles):
                        at = pl.ds(tile * LANES, LANES)
                        combined = digits[source, 0, rows, at] * keys[key, 0, poly, limbs, at]
                        for part in range(1, parts):
                            combined = combined + digits[source, part, rows, at] * keys[key, part, poly, limbs, at]
                        quotient = jnp.floor(combined * inverse)
                        remainder = combined - quotient * modulus
                        rolled[:, pl.ds((pad + tile) * LANES, LANES)] = pltpu.roll(remainder, turn, 1)
                    for tile in range(pad + tiles):
                        start = pl.multiple_of((skipped + tile) * LANES, LANES)
                        after = pl.multiple_of((skipped + tile + 1) * LANES, LANES)
                        moved = jnp.where(from_this, rolled[:, pl.ds(start, LANES)], rolled[:, pl.ds(after, LANES)])
                        if tile < pad:
                            at = pl.ds(tile * LANES, LANES)
                            tail[place, poly, rows, at] = tail[place, poly, rows, at] + moved
                        else:
                            at = pl.ds((tile - pad) * LANES, LANES)
                            resident[place, poly, rows, at] = resident[place, poly, rows, at] + moved

    def add_step(step, carry):
        key = step // len(blocks)
        block = step - key * len(blocks)
        if load:
            pl.when((block == 0) & wanted(key))(lambda: copy(key).wait())

        add_key(key, block)
        return carry

    lax.fori_loop(0, len(blocks) * key_count, add_step, 0)


def products(digits, keys, requests, rotations, modulus, slots, blocks, local, load):
    key_count, parts, polys, _, columns = keys.shape
    count = len(slots)
    limbs = len(blocks) * ROWS
    pad = WIDEST // LANES
    work = count * key_count * polys * limbs * columns
    scratch = [pltpu.VMEM((ROWS, columns + 2 * pad * LANES + LANES), jnp.float32)]
    if load:
        scratch.append(pltpu.VMEM((key_count, parts, polys, limbs, columns), jnp.float32))
        scratch.append(pltpu.SemaphoreType.DMA((key_count,)))
        keys = pltpu.with_memory_space_constraint(keys, pltpu.HBM)
    return pl.pallas_call(
        functools.partial(products_kernel, slots, blocks, local, load),
        out_shape=[
            jax.ShapeDtypeStruct((count, polys, limbs, WIDEST), jnp.float32),
            jax.ShapeDtypeStruct((count, polys, limbs, columns), jnp.float32),
        ],
        in_specs=[SMEM, SMEM, VMEM, pl.BlockSpec(memory_space=pltpu.HBM) if load else VMEM, VMEM],
        out_specs=[VMEM, VMEM],
        scratch_shapes=scratch,
        compiler_params=pltpu.CompilerParams(vmem_limit_bytes=20 << 20),
        cost_estimate=pl.CostEstimate(
            flops=20 * work,
            transcendentals=0,
            bytes_accessed=4 * (key_count * parts * polys * limbs * columns + count * limbs * columns * (parts + polys)),
        ),
        name="products",
    )(requests, rotations, digits, keys, modulus)


def add_tail_kernel(arrived, held, out):
    columns = held.shape[-1]
    at = pl.ds(columns - WIDEST, WIDEST)
    out[:, :, :, at] = held[:, :, :, at] + arrived[...]


def add_tail(resident, arrived):
    return pl.pallas_call(
        add_tail_kernel,
        out_shape=jax.ShapeDtypeStruct(resident.shape, jnp.float32),
        in_specs=[VMEM, VMEM],
        out_specs=VMEM,
        input_output_aliases={1: 0},
        compiler_params=pltpu.CompilerParams(vmem_limit_bytes=8 << 20),
        name="add_tail",
    )(arrived, resident)


def reduce_mod(amount, modulus):
    quotient = jnp.floor(amount * (1.0 / modulus))
    remainder = amount - quotient * modulus
    remainder = jnp.where(remainder < 0, remainder + modulus, remainder)
    return jnp.where(remainder >= modulus, remainder - modulus, remainder)


def sums_kernel(owners, groups, ciphers, key_count, requests, modulus, *refs):
    parts, out = refs[: len(owners)], refs[len(owners)]
    cipher = pl.program_id(1)
    out[...] = jnp.zeros_like(out)
    for part, (steps, slots) in zip(parts, owners):
        chosen = slot_ciphers(requests, ciphers, key_count, group_after(steps, groups))
        for place, slot in enumerate(slots):

            @pl.when(chosen[slot] == cipher)
            def _():
                out[...] = out[...] + part[place]

    wide = modulus[:, :1]
    out[...] = reduce_mod(out[...], wide) / wide


def sums(parts, owners, requests, modulus, ciphers):
    polys, limbs, columns = parts[0].shape[1:]
    groups = lax.axis_size("grp")
    key_count = requests.shape[1] // groups
    return pl.pallas_call(
        functools.partial(sums_kernel, owners, groups, ciphers, key_count),
        out_shape=jax.ShapeDtypeStruct((ciphers, polys, limbs, columns), jnp.float32),
        grid_spec=pltpu.PrefetchScalarGridSpec(
            num_scalar_prefetch=1,
            grid=(limbs // ROWS, ciphers),
            in_specs=[pl.BlockSpec((ROWS, LANES), lambda block, cipher, *_: (block, 0))]
            + [
                pl.BlockSpec((part.shape[0], polys, ROWS, columns), lambda block, cipher, *_: (0, 0, block, 0))
                for part in parts
            ],
            out_specs=pl.BlockSpec(
                (pl.Squeezed(), polys, ROWS, columns), lambda block, cipher, *_: (cipher, 0, block, 0)
            ),
        ),
        compiler_params=pltpu.CompilerParams(
            dimension_semantics=("arbitrary", "arbitrary"), vmem_limit_bytes=24 << 20
        ),
        name="sums",
    )(requests, modulus, *parts)


def orders_of(requests, groups):
    ciphers, columns = requests.shape
    key_count = columns // groups
    bits = key_count.bit_length()
    asks = requests[...]
    row = lax.broadcasted_iota(jnp.int32, asks.shape, 0)
    owner = lax.broadcasted_iota(jnp.int32, asks.shape, 1) // key_count
    me = group_after(0, groups)
    after = group_after(1, groups)
    place = jnp.where(owner == me, 0, ciphers) + row
    code = jnp.sum(jnp.where((owner == me) | (owner == after), asks << (place * bits), 0))
    flags = [
        ((code >> (place * bits)) & ((1 << bits) - 1) > 0).astype(jnp.int32) for place in range(2 * ciphers)
    ]
    return ranked(flags[:ciphers]), ranked(flags[ciphers:]), flags[:ciphers]


def finish_kernel(ranks, blocks, groups, pieces, tailed, requests, modulus, local, *refs):
    parts, (out, done, sems) = refs[:pieces], refs[-3:]
    tails = refs[pieces] if tailed else None
    polys, _, columns = out.shape[1:]
    ours, theirs, _ = orders_of(requests, groups)
    stores = []
    for at, rank in enumerate(ranks):
        cipher = theirs[rank]
        weights = [jnp.where(ours[slot] == cipher, 1.0, 0.0) for slot in range(CAP)]
        for which, block in enumerate(blocks):
            rows = pl.ds(block * ROWS, ROWS)
            here = pl.ds(which * ROWS, ROWS)
            wide = modulus[rows, :1]
            for poly in range(polys):
                total = local[0, poly, rows, :] * weights[0]
                for slot in range(1, CAP):
                    total = total + local[slot, poly, rows, :] * weights[slot]
                if pieces:
                    total = total + parts[which][0, poly]
                if tailed:
                    last = columns - WIDEST
                    wrapped = total[:, last:] + tails[0, poly, here, :]
                    done[at, poly, here, pl.ds(0, last)] = reduce_mod(total[:, :last], wide) / wide
                    done[at, poly, here, pl.ds(last, WIDEST)] = reduce_mod(wrapped, wide) / wide
                else:
                    done[at, poly, here, :] = reduce_mod(total, wide) / wide
                stores.append(
                    pltpu.make_async_copy(done.at[at, poly, here], out.at[cipher, poly, rows], sems.at[len(stores)])
                )
                stores[-1].start()
    for store in stores:
        store.wait()


def finish(local, requests, modulus, ciphers, ranks, blocks, parts=(), before=None, tails=None):
    _, polys, _, columns = local.shape
    hbm = pl.BlockSpec(memory_space=pltpu.HBM)
    limbs = modulus.shape[0]
    work = len(ranks) * polys * len(blocks) * ROWS * columns
    more = [*parts] + ([] if tails is None else [tails])
    specs = [VMEM] * (3 + len(more))
    if before is not None:
        more, specs = more + [before], specs + [hbm]
    return pl.pallas_call(
        functools.partial(finish_kernel, ranks, blocks, lax.axis_size("grp"), len(parts), tails is not None),
        out_shape=jax.ShapeDtypeStruct((ciphers, polys, limbs, columns), jnp.float32),
        in_specs=specs,
        out_specs=hbm,
        scratch_shapes=[
            pltpu.VMEM((len(ranks), polys, len(blocks) * ROWS, columns), jnp.float32),
            pltpu.SemaphoreType.DMA((len(ranks) * polys * len(blocks),)),
        ],
        input_output_aliases={} if before is None else {len(specs) - 1: 0},
        compiler_params=pltpu.CompilerParams(vmem_limit_bytes=8 << 20),
        cost_estimate=pl.CostEstimate(flops=20 * work, transcendentals=0, bytes_accessed=12 * work),
        name="finish",
    )(requests, modulus, local, *more)


def per_device(digits, keys, requests, rotations, moduli):
    modulus = jnp.broadcast_to(moduli.astype(jnp.float32)[:, None], (digits.shape[2], LANES))
    way = key_switch_pair if lax.axis_size("grp") == 2 else key_switch_any
    return way(digits, keys, requests, rotations, modulus)


def key_switch_any(digits, keys, requests, rotations, modulus):
    groups = lax.axis_size("grp")
    blocks = tuple(range(digits.shape[2] // ROWS))
    slots = tuple(range(CAP))
    tail, resident = products(digits, keys, requests, rotations, modulus, slots, blocks, True, True)
    parts = [add_tail(resident, shifted(tail, "limb", -1))]
    owners = [(0, slots)]
    for steps in range(1, groups):
        asked = shifted(requests, "grp", steps)
        for slot in slots:
            picked = gather(digits, requests, steps, tuple((slot, block) for block in blocks))
            back = []
            for block in blocks:
                arrived = shifted(picked[block], "grp", steps)
                tail, resident = products(
                    arrived[None], keys, asked, rotations, modulus, (slot,), (block,), False, True
                )
                back.append(shifted(add_tail(resident, shifted(tail, "limb", -1)), "grp", -steps))
            parts.append(jnp.concatenate(back, axis=2))
            owners.append((steps, (slot,)))
    return sums(parts, tuple(owners), requests, modulus, digits.shape[0])


def key_switch_pair(digits, keys, requests, rotations, modulus):
    blocks = tuple(range(digits.shape[2] // ROWS))
    slots = tuple(range(CAP))
    key_count = keys.shape[0]
    both = [(0, 1), (1, 0)]
    turns = [(slot, block) for slot in slots for block in blocks]
    picked = {turns[0]: gather(digits, requests, 1, (turns[0],))[0]}
    picked.update(zip(turns[1:], gather(digits, requests, 1, tuple(turns[1:]))))
    sent = {}
    for block in blocks:
        sent[0, block] = lax.ppermute(picked[0, block], "grp", both)
    asked = shifted(requests, "grp", 1)
    tail, resident = products(digits, keys, requests, rotations, modulus, slots, blocks, True, True)
    me = lax.axis_index("grp")
    rightward = jnp.where(me == 0, requests, asked)[:, key_count:]
    leftward = jnp.where(me == 0, asked, requests)[:, :key_count]
    base = digits.shape[0] + 1
    counts = jnp.sum(jnp.max(rightward, axis=1) + base * jnp.max(leftward, axis=1))
    two_right = counts % base > 1
    two_left = counts // base > 1
    case = jnp.where(two_right == two_left, 0, jnp.where(two_right, 1, 2))
    ahead = joined(*remote(sent[0, 0], keys, asked, rotations, modulus, 0, 0))

    def branch(pairs):
        def run(*operands):
            return exchange((both, pairs), *operands)

        return run

    branches = [branch(pairs) for pairs in (both, [(0, 1)], [(1, 0)])]
    operands = (ahead, [picked[turn] for turn in turns[len(blocks) :]], [sent[0, block] for block in blocks[1:]], tail, resident)
    return lax.switch(case, branches, *operands, keys, requests, asked, rotations, modulus)


def remote(arrived, keys, asked, rotations, modulus, slot, block):
    return products(arrived[None], keys, asked, rotations, modulus, (slot,), (block,), False, slot == 0)


def joined(tail, resident):
    wrapped = shifted(tail, "limb", -1)
    return add_tail(resident, wrapped)


def exchange(pairs, ahead, picked, arrived, tail, resident, keys, requests, asked, rotations, modulus):
    ciphers = requests.shape[0]
    blocks = resident.shape[2] // ROWS
    turns = [(slot, block) for slot in range(CAP) for block in range(blocks)]
    sent = dict(zip(turns[1:blocks], arrived))
    for (slot, block), piece in zip(turns[blocks:], picked):
        sent[slot, block] = lax.ppermute(piece, "grp", pairs[slot])
    local = joined(tail, resident)
    result = finish(local, requests, modulus, ciphers, tuple(range(CAP, ciphers)), tuple(range(blocks)))
    back = {}
    late = []
    for turn in turns:
        slot, block = turn
        ways = [(target, source) for source, target in pairs[slot]]
        if turn == turns[0]:
            whole = ahead
        else:
            tail, whole = remote(sent[turn], keys, asked, rotations, modulus, slot, block)
            if len(ways) == 2:
                whole = joined(tail, whole)
            else:
                late.append(tail)
        if len(late) == blocks:
            tails = lax.ppermute(jnp.concatenate(late, axis=2), "grp", ways)
            tails = shifted(tails, "limb", -1)
        back[turn] = lax.ppermute(whole, "grp", ways)
    for slot, block in turns:
        if len(pairs[slot]) == 2:
            result = finish(local, requests, modulus, ciphers, (slot,), (block,), (back[slot, block],), result)
    if late:
        pieces = tuple(back[turn] for turn in turns[blocks:])
        result = finish(
            local, requests, modulus, ciphers, (CAP - 1,), tuple(range(blocks)), pieces, result, tails
        )
    return result


def solution(mesh):
    in_specs = (
        P("grp", None, None, "limb"),
        P("grp", None, None, None, "limb"),
        P("grp", None),
        P(),
        P(),
    )
    out_specs = P("grp", None, None, "limb")
    return jax.shard_map(
        per_device, mesh=mesh, in_specs=in_specs, out_specs=out_specs, check_vma=False
    )
```

```python
import functools

import jax
import jax.numpy as jnp
from jax import lax
from jax.experimental import pallas as pl
from jax.experimental.pallas import tpu as pltpu
from jax.sharding import PartitionSpec as P

RMAX = 256
CAP = 2
WIDEST = 2 * RMAX
LANES = 128
ROWS = 8
SMEM = pl.BlockSpec(memory_space=pltpu.SMEM)
VMEM = pl.BlockSpec(memory_space=pltpu.VMEM)


def shifted(value, axis, steps):
    count = lax.axis_size(axis)
    pairs = [(source, (source + steps) % count) for source in range(count)]
    return lax.ppermute(value, axis, pairs)


def slot_ciphers(requests, ciphers, key_count, owner):
    needed = []
    for cipher in range(ciphers):
        flag = requests[cipher, owner * key_count]
        for key in range(1, key_count):
            flag = flag | requests[cipher, owner * key_count + key]
        needed.append(flag)
    return ranked(needed)


def ranked(needed):
    slots = [jnp.int32(0)] * len(needed)
    rank = jnp.int32(0)
    for want in (1, 0):
        for cipher in range(len(needed)):
            here = needed[cipher] == want
            for slot in range(len(needed)):
                slots[slot] = jnp.where(here & (rank == slot), cipher, slots[slot])
            rank = rank + here.astype(jnp.int32)
    return slots


def group_after(steps, groups):
    return lax.rem(lax.axis_index("grp") + steps, groups)


def gather_kernel(wanted, cuts, steps, groups, requests, digits, *refs):
    outs, sems = refs[: len(wanted)], refs[len(wanted)]
    ciphers, parts, _, columns = digits.shape
    chosen = slot_ciphers(requests, ciphers, requests.shape[1] // groups, group_after(steps, groups))
    width = columns // cuts
    loads = []
    for out, (slot, block) in zip(outs, wanted):
        for part in range(parts):
            for cut in range(cuts):
                at = pl.ds(cut * width, width)
                source = digits.at[chosen[slot], part, pl.ds(block * ROWS, ROWS), at]
                loads.append(pltpu.make_async_copy(source, out.at[part, :, at], sems.at[len(loads)]))
    for load in loads:
        load.start()
    for load in loads:
        load.wait()


def gather(digits, requests, steps, wanted, cuts=1):
    parts, _, columns = digits.shape[1:]
    return pl.pallas_call(
        functools.partial(gather_kernel, wanted, cuts, steps, lax.axis_size("grp")),
        out_shape=[jax.ShapeDtypeStruct((parts, ROWS, columns), jnp.float32)] * len(wanted),
        in_specs=[SMEM, pl.BlockSpec(memory_space=pltpu.HBM)],
        out_specs=[VMEM] * len(wanted),
        scratch_shapes=[pltpu.SemaphoreType.DMA((cuts * parts * len(wanted),))],
        compiler_params=pltpu.CompilerParams(vmem_limit_bytes=4 << 20),
        cost_estimate=pl.CostEstimate(
            flops=0, transcendentals=0, bytes_accessed=8 * len(wanted) * parts * ROWS * columns
        ),
        name="gather",
    )(requests, pltpu.with_memory_space_constraint(digits, pltpu.HBM))


def products_kernel(slots, blocks, local, load, requests, rotations, digits, keys, modulus_ref, tail, resident, *refs):
    key_count, parts, polys, _, columns = keys.shape
    ciphers = requests.shape[0]
    pad = WIDEST // LANES
    tiles = columns // LANES
    rolled = refs[0]
    me = lax.axis_index("grp")
    chosen = slot_ciphers(requests, ciphers, key_count, me)
    first = blocks[0]

    def wanted(key):
        flag = requests[chosen[slots[0]], me * key_count + key]
        for slot in slots[1:]:
            flag = flag | requests[chosen[slot], me * key_count + key]
        return flag > 0

    if load:
        whole, (keys, sems) = keys, refs[1:]
        here = pl.ds(blocks[0] * ROWS, len(blocks) * ROWS)
        first = 0

        def copy(key):
            return pltpu.make_async_copy(whole.at[key, :, :, here], keys.at[key], sems.at[key])

        for key in range(key_count):
            pl.when(wanted(key))(copy(key).start)

    tail[...] = jnp.zeros_like(tail)
    resident[...] = jnp.zeros_like(resident)
    rolled[...] = jnp.zeros_like(rolled)
    lane = lax.broadcasted_iota(jnp.int32, (ROWS, LANES), 1)

    def add_key(key, block):
        rows = pl.ds(pl.multiple_of(block * ROWS, ROWS), ROWS)
        limbs = pl.ds(pl.multiple_of((first + block) * ROWS, ROWS), ROWS)
        amount = 2 * rotations[me * key_count + key]
        skipped = amount // LANES
        within = amount - skipped * LANES
        turn = lax.rem(LANES - within, LANES)
        from_this = lane < LANES - within
        modulus = modulus_ref[pl.ds(pl.multiple_of((blocks[0] + block) * ROWS, ROWS), ROWS), :]
        inverse = 1.0 / modulus
        for place, slot in enumerate(slots):
            source = chosen[slot] if local else place

            @pl.when(requests[chosen[slot], me * key_count + key] > 0)
            def _():
                for poly in range(polys):
                    for tile in range(tiles):
                        at = pl.ds(tile * LANES, LANES)
                        combined = digits[source, 0, rows, at] * keys[key, 0, poly, limbs, at]
                        for part in range(1, parts):
                            combined = combined + digits[source, part, rows, at] * keys[key, part, poly, limbs, at]
                        quotient = jnp.floor(combined * inverse)
                        remainder = combined - quotient * modulus
                        rolled[:, pl.ds((pad + tile) * LANES, LANES)] = pltpu.roll(remainder, turn, 1)
                    for tile in range(pad + tiles):
                        start = pl.multiple_of((skipped + tile) * LANES, LANES)
                        after = pl.multiple_of((skipped + tile + 1) * LANES, LANES)
                        moved = jnp.where(from_this, rolled[:, pl.ds(start, LANES)], rolled[:, pl.ds(after, LANES)])
                        if tile < pad:
                            at = pl.ds(tile * LANES, LANES)
                            tail[place, poly, rows, at] = tail[place, poly, rows, at] + moved
                        else:
                            at = pl.ds((tile - pad) * LANES, LANES)
                            resident[place, poly, rows, at] = resident[place, poly, rows, at] + moved

    def add_step(step, carry):
        key = step // len(blocks)
        block = step - key * len(blocks)
        if load:
            pl.when((block == 0) & wanted(key))(lambda: copy(key).wait())

        add_key(key, block)
        return carry

    lax.fori_loop(0, len(blocks) * key_count, add_step, 0)


def products(digits, keys, requests, rotations, modulus, slots, blocks, local, load):
    key_count, parts, polys, _, columns = keys.shape
    count = len(slots)
    limbs = len(blocks) * ROWS
    pad = WIDEST // LANES
    work = count * key_count * polys * limbs * columns
    scratch = [pltpu.VMEM((ROWS, columns + 2 * pad * LANES + LANES), jnp.float32)]
    if load:
        scratch.append(pltpu.VMEM((key_count, parts, polys, limbs, columns), jnp.float32))
        scratch.append(pltpu.SemaphoreType.DMA((key_count,)))
        keys = pltpu.with_memory_space_constraint(keys, pltpu.HBM)
    return pl.pallas_call(
        functools.partial(products_kernel, slots, blocks, local, load),
        out_shape=[
            jax.ShapeDtypeStruct((count, polys, limbs, WIDEST), jnp.float32),
            jax.ShapeDtypeStruct((count, polys, limbs, columns), jnp.float32),
        ],
        in_specs=[SMEM, SMEM, VMEM, pl.BlockSpec(memory_space=pltpu.HBM) if load else VMEM, VMEM],
        out_specs=[VMEM, VMEM],
        scratch_shapes=scratch,
        compiler_params=pltpu.CompilerParams(vmem_limit_bytes=20 << 20),
        cost_estimate=pl.CostEstimate(
            flops=20 * work,
            transcendentals=0,
            bytes_accessed=4 * (key_count * parts * polys * limbs * columns + count * limbs * columns * (parts + polys)),
        ),
        name="products",
    )(requests, rotations, digits, keys, modulus)


def add_tail_kernel(arrived, held, out):
    columns = held.shape[-1]
    at = pl.ds(columns - WIDEST, WIDEST)
    out[:, :, :, at] = held[:, :, :, at] + arrived[...]


def add_tail(resident, arrived):
    return pl.pallas_call(
        add_tail_kernel,
        out_shape=jax.ShapeDtypeStruct(resident.shape, jnp.float32),
        in_specs=[VMEM, VMEM],
        out_specs=VMEM,
        input_output_aliases={1: 0},
        compiler_params=pltpu.CompilerParams(vmem_limit_bytes=8 << 20),
        name="add_tail",
    )(arrived, resident)


def reduce_mod(amount, modulus):
    quotient = jnp.floor(amount * (1.0 / modulus))
    remainder = amount - quotient * modulus
    remainder = jnp.where(remainder < 0, remainder + modulus, remainder)
    return jnp.where(remainder >= modulus, remainder - modulus, remainder)


def sums_kernel(owners, groups, ciphers, key_count, requests, modulus, *refs):
    parts, out = refs[: len(owners)], refs[len(owners)]
    cipher = pl.program_id(1)
    out[...] = jnp.zeros_like(out)
    for part, (steps, slots) in zip(parts, owners):
        chosen = slot_ciphers(requests, ciphers, key_count, group_after(steps, groups))
        for place, slot in enumerate(slots):

            @pl.when(chosen[slot] == cipher)
            def _():
                out[...] = out[...] + part[place]

    wide = modulus[:, :1]
    out[...] = reduce_mod(out[...], wide) / wide


def sums(parts, owners, requests, modulus, ciphers):
    polys, limbs, columns = parts[0].shape[1:]
    groups = lax.axis_size("grp")
    key_count = requests.shape[1] // groups
    return pl.pallas_call(
        functools.partial(sums_kernel, owners, groups, ciphers, key_count),
        out_shape=jax.ShapeDtypeStruct((ciphers, polys, limbs, columns), jnp.float32),
        grid_spec=pltpu.PrefetchScalarGridSpec(
            num_scalar_prefetch=1,
            grid=(limbs // ROWS, ciphers),
            in_specs=[pl.BlockSpec((ROWS, LANES), lambda block, cipher, *_: (block, 0))]
            + [
                pl.BlockSpec((part.shape[0], polys, ROWS, columns), lambda block, cipher, *_: (0, 0, block, 0))
                for part in parts
            ],
            out_specs=pl.BlockSpec(
                (pl.Squeezed(), polys, ROWS, columns), lambda block, cipher, *_: (cipher, 0, block, 0)
            ),
        ),
        compiler_params=pltpu.CompilerParams(
            dimension_semantics=("arbitrary", "arbitrary"), vmem_limit_bytes=24 << 20
        ),
        name="sums",
    )(requests, modulus, *parts)


def orders_of(requests, groups):
    ciphers, columns = requests.shape
    key_count = columns // groups
    bits = key_count.bit_length()
    asks = requests[...]
    row = lax.broadcasted_iota(jnp.int32, asks.shape, 0)
    owner = lax.broadcasted_iota(jnp.int32, asks.shape, 1) // key_count
    me = group_after(0, groups)
    after = group_after(1, groups)
    place = jnp.where(owner == me, 0, ciphers) + row
    code = jnp.sum(jnp.where((owner == me) | (owner == after), asks << (place * bits), 0))
    flags = [
        ((code >> (place * bits)) & ((1 << bits) - 1) > 0).astype(jnp.int32) for place in range(2 * ciphers)
    ]
    return ranked(flags[:ciphers]), ranked(flags[ciphers:]), flags[:ciphers]


def finish_kernel(ranks, blocks, groups, pieces, tailed, requests, modulus, local, *refs):
    parts, (out, done, sems) = refs[:pieces], refs[-3:]
    tails = refs[pieces] if tailed else None
    polys, _, columns = out.shape[1:]
    ours, theirs, _ = orders_of(requests, groups)
    stores = []
    for at, rank in enumerate(ranks):
        cipher = theirs[rank]
        weights = [jnp.where(ours[slot] == cipher, 1.0, 0.0) for slot in range(CAP)]
        for which, block in enumerate(blocks):
            rows = pl.ds(block * ROWS, ROWS)
            here = pl.ds(which * ROWS, ROWS)
            wide = modulus[rows, :1]
            for poly in range(polys):
                total = local[0, poly, rows, :] * weights[0]
                for slot in range(1, CAP):
                    total = total + local[slot, poly, rows, :] * weights[slot]
                if pieces:
                    total = total + parts[which][0, poly]
                if tailed:
                    last = columns - WIDEST
                    wrapped = total[:, last:] + tails[0, poly, here, :]
                    done[at, poly, here, pl.ds(0, last)] = reduce_mod(total[:, :last], wide) / wide
                    done[at, poly, here, pl.ds(last, WIDEST)] = reduce_mod(wrapped, wide) / wide
                else:
                    done[at, poly, here, :] = reduce_mod(total, wide) / wide
                stores.append(
                    pltpu.make_async_copy(done.at[at, poly, here], out.at[cipher, poly, rows], sems.at[len(stores)])
                )
                stores[-1].start()
    for store in stores:
        store.wait()


def finish(local, requests, modulus, ciphers, ranks, blocks, parts=(), before=None, tails=None):
    _, polys, _, columns = local.shape
    hbm = pl.BlockSpec(memory_space=pltpu.HBM)
    limbs = modulus.shape[0]
    work = len(ranks) * polys * len(blocks) * ROWS * columns
    more = [*parts] + ([] if tails is None else [tails])
    specs = [VMEM] * (3 + len(more))
    if before is not None:
        more, specs = more + [before], specs + [hbm]
    return pl.pallas_call(
        functools.partial(finish_kernel, ranks, blocks, lax.axis_size("grp"), len(parts), tails is not None),
        out_shape=jax.ShapeDtypeStruct((ciphers, polys, limbs, columns), jnp.float32),
        in_specs=specs,
        out_specs=hbm,
        scratch_shapes=[
            pltpu.VMEM((len(ranks), polys, len(blocks) * ROWS, columns), jnp.float32),
            pltpu.SemaphoreType.DMA((len(ranks) * polys * len(blocks),)),
        ],
        input_output_aliases={} if before is None else {len(specs) - 1: 0},
        compiler_params=pltpu.CompilerParams(vmem_limit_bytes=8 << 20),
        cost_estimate=pl.CostEstimate(flops=20 * work, transcendentals=0, bytes_accessed=12 * work),
        name="finish",
    )(requests, modulus, local, *more)


def per_device(digits, keys, requests, rotations, moduli):
    modulus = jnp.broadcast_to(moduli.astype(jnp.float32)[:, None], (digits.shape[2], LANES))
    way = key_switch_pair if lax.axis_size("grp") == 2 else key_switch_any
    return way(digits, keys, requests, rotations, modulus)


def key_switch_any(digits, keys, requests, rotations, modulus):
    groups = lax.axis_size("grp")
    blocks = tuple(range(digits.shape[2] // ROWS))
    slots = tuple(range(CAP))
    tail, resident = products(digits, keys, requests, rotations, modulus, slots, blocks, True, True)
    parts = [add_tail(resident, shifted(tail, "limb", -1))]
    owners = [(0, slots)]
    for steps in range(1, groups):
        asked = shifted(requests, "grp", steps)
        for slot in slots:
            picked = gather(digits, requests, steps, tuple((slot, block) for block in blocks))
            back = []
            for block in blocks:
                arrived = shifted(picked[block], "grp", steps)
                tail, resident = products(
                    arrived[None], keys, asked, rotations, modulus, (slot,), (block,), False, True
                )
                back.append(shifted(add_tail(resident, shifted(tail, "limb", -1)), "grp", -steps))
            parts.append(jnp.concatenate(back, axis=2))
            owners.append((steps, (slot,)))
    return sums(parts, tuple(owners), requests, modulus, digits.shape[0])


def key_switch_pair(digits, keys, requests, rotations, modulus):
    blocks = tuple(range(digits.shape[2] // ROWS))
    slots = tuple(range(CAP))
    key_count = keys.shape[0]
    both = [(0, 1), (1, 0)]
    turns = [(slot, block) for slot in slots for block in blocks]
    picked = {turns[0]: gather(digits, requests, 1, (turns[0],), 4)[0]}
    picked.update(zip(turns[1:], gather(digits, requests, 1, tuple(turns[1:]))))
    sent = {}
    for block in blocks:
        sent[0, block] = lax.ppermute(picked[0, block], "grp", both)
    asked = shifted(requests, "grp", 1)
    tail, resident = products(digits, keys, requests, rotations, modulus, slots, blocks, True, True)
    me = lax.axis_index("grp")
    rightward = jnp.where(me == 0, requests, asked)[:, key_count:]
    leftward = jnp.where(me == 0, asked, requests)[:, :key_count]
    bits = digits.shape[0].bit_length()
    counts = jnp.sum(jnp.max(rightward, axis=1) + (jnp.max(leftward, axis=1) << bits))
    two_right = counts & ((1 << bits) - 1) > 1
    two_left = counts >> bits > 1
    case = jnp.where(two_right == two_left, 0, jnp.where(two_right, 1, 2))
    ahead = joined(*remote(sent[0, 0], keys, asked, rotations, modulus, 0, 0))

    def branch(pairs):
        def run(*operands):
            return exchange((both, pairs), *operands)

        return run

    branches = [branch(pairs) for pairs in (both, [(0, 1)], [(1, 0)])]
    operands = (ahead, [picked[turn] for turn in turns[len(blocks) :]], [sent[0, block] for block in blocks[1:]], tail, resident)
    return lax.switch(case, branches, *operands, keys, requests, asked, rotations, modulus)


def remote(arrived, keys, asked, rotations, modulus, slot, block):
    return products(arrived[None], keys, asked, rotations, modulus, (slot,), (block,), False, slot == 0)


def joined(tail, resident):
    wrapped = shifted(tail, "limb", -1)
    return add_tail(resident, wrapped)


def exchange(pairs, ahead, picked, arrived, tail, resident, keys, requests, asked, rotations, modulus):
    ciphers = requests.shape[0]
    blocks = resident.shape[2] // ROWS
    turns = [(slot, block) for slot in range(CAP) for block in range(blocks)]
    sent = dict(zip(turns[1:blocks], arrived))
    for (slot, block), piece in zip(turns[blocks:], picked):
        sent[slot, block] = lax.ppermute(piece, "grp", pairs[slot])
    local = joined(tail, resident)
    result = finish(local, requests, modulus, ciphers, tuple(range(CAP, ciphers)), tuple(range(blocks)))
    back = {}
    late = []
    for turn in turns:
        slot, block = turn
        ways = [(target, source) for source, target in pairs[slot]]
        if turn == turns[0]:
            whole = ahead
        else:
            tail, whole = remote(sent[turn], keys, asked, rotations, modulus, slot, block)
            if len(ways) == 2:
                whole = joined(tail, whole)
            else:
                late.append(tail)
        if len(late) == blocks:
            tails = lax.ppermute(jnp.concatenate(late, axis=2), "grp", ways)
            tails = shifted(tails, "limb", -1)
        back[turn] = lax.ppermute(whole, "grp", ways)
    for slot, block in turns:
        if len(pairs[slot]) == 2:
            result = finish(local, requests, modulus, ciphers, (slot,), (block,), (back[slot, block],), result)
    if late:
        pieces = tuple(back[turn] for turn in turns[blocks:])
        result = finish(
            local, requests, modulus, ciphers, (CAP - 1,), tuple(range(blocks)), pieces, result, tails
        )
    return result


def solution(mesh):
    in_specs = (
        P("grp", None, None, "limb"),
        P("grp", None, None, None, "limb"),
        P("grp", None),
        P(),
        P(),
    )
    out_specs = P("grp", None, None, "limb")
    return jax.shard_map(
        per_device, mesh=mesh, in_specs=in_specs, out_specs=out_specs, check_vma=False
    )
```

```python
import functools

import jax
import jax.numpy as jnp
from jax import lax
from jax.experimental import pallas as pl
from jax.experimental.pallas import tpu as pltpu
from jax.sharding import PartitionSpec as P

RMAX = 256
CAP = 2
WIDEST = 2 * RMAX
LANES = 128
ROWS = 8
SMEM = pl.BlockSpec(memory_space=pltpu.SMEM)
VMEM = pl.BlockSpec(memory_space=pltpu.VMEM)


def shifted(value, axis, steps):
    count = lax.axis_size(axis)
    pairs = [(source, (source + steps) % count) for source in range(count)]
    return lax.ppermute(value, axis, pairs)


def slot_ciphers(requests, ciphers, key_count, owner):
    needed = []
    for cipher in range(ciphers):
        flag = requests[cipher, owner * key_count]
        for key in range(1, key_count):
            flag = flag | requests[cipher, owner * key_count + key]
        needed.append(flag)
    return ranked(needed)


def ranked(needed):
    slots = [jnp.int32(0)] * CAP
    rank = jnp.int32(0)
    for want in (1, 0):
        for cipher in range(len(needed)):
            here = needed[cipher] == want
            for slot in range(CAP):
                slots[slot] = jnp.where(here & (rank == slot), cipher, slots[slot])
            rank = rank + here.astype(jnp.int32)
    return slots


def group_after(steps, groups):
    return lax.rem(lax.axis_index("grp") + steps, groups)


def gather_kernel(wanted, cuts, steps, groups, requests, digits, *refs):
    outs, sems = refs[: len(wanted)], refs[len(wanted)]
    ciphers, parts, _, columns = digits.shape
    chosen = slot_ciphers(requests, ciphers, requests.shape[1] // groups, group_after(steps, groups))
    width = columns // cuts
    loads = []
    for out, (slot, block) in zip(outs, wanted):
        for part in range(parts):
            for cut in range(cuts):
                at = pl.ds(cut * width, width)
                source = digits.at[chosen[slot], part, pl.ds(block * ROWS, ROWS), at]
                loads.append(pltpu.make_async_copy(source, out.at[part, :, at], sems.at[len(loads)]))
    for load in loads:
        load.start()
    for load in loads:
        load.wait()


def gather(digits, requests, steps, wanted, cuts=1):
    parts, _, columns = digits.shape[1:]
    return pl.pallas_call(
        functools.partial(gather_kernel, wanted, cuts, steps, lax.axis_size("grp")),
        out_shape=[jax.ShapeDtypeStruct((parts, ROWS, columns), jnp.float32)] * len(wanted),
        in_specs=[SMEM, pl.BlockSpec(memory_space=pltpu.HBM)],
        out_specs=[VMEM] * len(wanted),
        scratch_shapes=[pltpu.SemaphoreType.DMA((cuts * parts * len(wanted),))],
        compiler_params=pltpu.CompilerParams(vmem_limit_bytes=4 << 20),
        cost_estimate=pl.CostEstimate(
            flops=0, transcendentals=0, bytes_accessed=8 * len(wanted) * parts * ROWS * columns
        ),
        name="gather_digits",
    )(requests, pltpu.with_memory_space_constraint(digits, pltpu.HBM))


def products_kernel(slots, blocks, local, requests, rotations, digits, keys, modulus_ref, tail, resident, rolled):
    key_count, parts, polys, _, columns = keys.shape
    ciphers = requests.shape[0]
    pad = WIDEST // LANES
    tiles = columns // LANES
    tail[...] = jnp.zeros_like(tail)
    resident[...] = jnp.zeros_like(resident)
    rolled[...] = jnp.zeros_like(rolled)
    lane = lax.broadcasted_iota(jnp.int32, (ROWS, LANES), 1)
    me = lax.axis_index("grp")
    chosen = slot_ciphers(requests, ciphers, key_count, me)

    def add_key(step, carry):
        block = step // key_count
        key = step - block * key_count
        rows = pl.ds(pl.multiple_of(block * ROWS, ROWS), ROWS)
        limbs = pl.ds(pl.multiple_of((blocks[0] + block) * ROWS, ROWS), ROWS)
        amount = 2 * rotations[me * key_count + key]
        skipped = amount // LANES
        within = amount - skipped * LANES
        turn = lax.rem(LANES - within, LANES)
        from_this = lane < LANES - within
        modulus = modulus_ref[limbs, :]
        inverse = 1.0 / modulus
        for place, slot in enumerate(slots):
            source = chosen[slot] if local else place

            @pl.when(requests[chosen[slot], me * key_count + key] > 0)
            def _():
                for poly in range(polys):
                    for tile in range(tiles):
                        at = pl.ds(tile * LANES, LANES)
                        combined = digits[source, 0, rows, at] * keys[key, 0, poly, limbs, at]
                        for part in range(1, parts):
                            combined = combined + digits[source, part, rows, at] * keys[key, part, poly, limbs, at]
                        quotient = jnp.floor(combined * inverse)
                        remainder = combined - quotient * modulus
                        rolled[:, pl.ds((pad + tile) * LANES, LANES)] = pltpu.roll(remainder, turn, 1)
                    for tile in range(pad + tiles):
                        start = pl.multiple_of((skipped + tile) * LANES, LANES)
                        after = pl.multiple_of((skipped + tile + 1) * LANES, LANES)
                        moved = jnp.where(from_this, rolled[:, pl.ds(start, LANES)], rolled[:, pl.ds(after, LANES)])
                        if tile < pad:
                            at = pl.ds(tile * LANES, LANES)
                            tail[place, poly, rows, at] = tail[place, poly, rows, at] + moved
                        else:
                            at = pl.ds((tile - pad) * LANES, LANES)
                            resident[place, poly, rows, at] = resident[place, poly, rows, at] + moved
        return carry

    lax.fori_loop(0, len(blocks) * key_count, add_key, 0)


def products(digits, keys, requests, rotations, modulus, slots, blocks, local):
    key_count, parts, polys, _, columns = keys.shape
    count = len(slots)
    limbs = len(blocks) * ROWS
    pad = WIDEST // LANES
    work = count * key_count * polys * limbs * columns
    return pl.pallas_call(
        functools.partial(products_kernel, slots, blocks, local),
        out_shape=[
            jax.ShapeDtypeStruct((count, polys, limbs, WIDEST), jnp.float32),
            jax.ShapeDtypeStruct((count, polys, limbs, columns), jnp.float32),
        ],
        in_specs=[SMEM, SMEM, VMEM, VMEM, VMEM],
        out_specs=[VMEM, VMEM],
        scratch_shapes=[pltpu.VMEM((ROWS, columns + 2 * pad * LANES + LANES), jnp.float32)],
        compiler_params=pltpu.CompilerParams(vmem_limit_bytes=20 << 20),
        cost_estimate=pl.CostEstimate(
            flops=20 * work, transcendentals=0, bytes_accessed=4 * (key_count * parts * polys * limbs * columns + count * limbs * columns * (parts + polys))
        ),
        name="products",
    )(requests, rotations, digits, keys, modulus)


def add_tail_kernel(arrived, held, out):
    columns = held.shape[-1]
    at = pl.ds(columns - WIDEST, WIDEST)
    out[:, :, :, at] = held[:, :, :, at] + arrived[...]


def add_tail(resident, arrived):
    return pl.pallas_call(
        add_tail_kernel,
        out_shape=jax.ShapeDtypeStruct(resident.shape, jnp.float32),
        in_specs=[VMEM, VMEM],
        out_specs=VMEM,
        input_output_aliases={1: 0},
        compiler_params=pltpu.CompilerParams(vmem_limit_bytes=8 << 20),
        name="add_tail",
    )(arrived, resident)


def reduce_mod(amount, modulus):
    quotient = jnp.floor(amount * (1.0 / modulus))
    remainder = amount - quotient * modulus
    remainder = jnp.where(remainder < 0, remainder + modulus, remainder)
    return jnp.where(remainder >= modulus, remainder - modulus, remainder)


def sums_kernel(owners, groups, ciphers, key_count, keep, requests, modulus, *refs):
    parts = refs[: len(owners)]
    out = refs[len(owners)]
    cipher = pl.program_id(1)
    out[...] = jnp.zeros_like(out)
    for part, (steps, slots) in zip(parts, owners):
        chosen = slot_ciphers(requests, ciphers, key_count, group_after(steps, groups))
        for place, slot in enumerate(slots):

            @pl.when(chosen[slot] == cipher)
            def _():
                out[...] = out[...] + part[place]

    if keep:
        held = refs[len(owners) + 1]
        chosen = slot_ciphers(requests, ciphers, key_count, group_after(groups - 1, groups))
        for slot in range(CAP):

            @pl.when(chosen[slot] == cipher)
            def _():
                held[slot] = out[...]

    wide = modulus[:, :1]
    out[...] = reduce_mod(out[...], wide) / wide


def sums(parts, owners, requests, modulus, ciphers, keep):
    polys, limbs, columns = parts[0].shape[1:]
    groups = lax.axis_size("grp")
    key_count = requests.shape[1] // groups
    shapes = [jax.ShapeDtypeStruct((ciphers, polys, limbs, columns), jnp.float32)]
    specs = [pl.BlockSpec((pl.Squeezed(), polys, ROWS, columns), lambda block, cipher, *_: (cipher, 0, block, 0))]
    if keep:
        shapes.append(jax.ShapeDtypeStruct((CAP, polys, limbs, columns), jnp.float32))
        specs.append(pl.BlockSpec((CAP, polys, ROWS, columns), lambda block, cipher, *_: (0, 0, block, 0)))
    return pl.pallas_call(
        functools.partial(sums_kernel, owners, groups, ciphers, key_count, keep),
        out_shape=shapes,
        grid_spec=pltpu.PrefetchScalarGridSpec(
            num_scalar_prefetch=1,
            grid=(limbs // ROWS, ciphers),
            in_specs=[pl.BlockSpec((ROWS, LANES), lambda block, cipher, *_: (block, 0))]
            + [
                pl.BlockSpec((part.shape[0], polys, ROWS, columns), lambda block, cipher, *_: (0, 0, block, 0))
                for part in parts
            ],
            out_specs=specs,
        ),
        compiler_params=pltpu.CompilerParams(
            dimension_semantics=("arbitrary", "arbitrary"), vmem_limit_bytes=24 << 20
        ),
        cost_estimate=pl.CostEstimate(
            flops=20 * ciphers * polys * limbs * columns,
            transcendentals=0,
            bytes_accessed=4 * (ciphers + 2 + 2 * len(parts)) * polys * limbs * columns,
        ),
        name="sums",
    )(requests, modulus, *parts)


def finish_kernel(slot, block, groups, requests, modulus, part, held, before, out, done, sems):
    ciphers, polys, _, _ = out.shape
    key_count = requests.shape[1] // groups
    rows = pl.ds(block * ROWS, ROWS)
    wide = modulus[rows, :1]
    for poly in range(polys):
        done[poly] = reduce_mod(held[slot, poly, rows, :] + part[0, poly], wide) / wide
    asks = requests[...]
    column = lax.broadcasted_iota(jnp.int32, asks.shape, 1) // key_count
    row = lax.broadcasted_iota(jnp.int32, asks.shape, 0)
    asks = jnp.where(column == group_after(groups - 1, groups), asks, 0)
    needed = [jnp.max(jnp.where(row == cipher, asks, 0)) for cipher in range(ciphers)]
    cipher = ranked(needed)[slot]
    stores = [
        pltpu.make_async_copy(done.at[poly], out.at[cipher, poly, rows], sems.at[poly]) for poly in range(polys)
    ]
    for store in stores:
        store.start()
    for store in stores:
        store.wait()


def finish(part, held, result, requests, modulus, slot, block):
    _, polys, _, columns = result.shape
    groups = lax.axis_size("grp")
    hbm = pl.BlockSpec(memory_space=pltpu.HBM)
    return pl.pallas_call(
        functools.partial(finish_kernel, slot, block, groups),
        out_shape=jax.ShapeDtypeStruct(result.shape, jnp.float32),
        in_specs=[VMEM, VMEM, VMEM, VMEM, hbm],
        out_specs=hbm,
        scratch_shapes=[pltpu.VMEM((polys, ROWS, columns), jnp.float32), pltpu.SemaphoreType.DMA((polys,))],
        input_output_aliases={4: 0},
        compiler_params=pltpu.CompilerParams(vmem_limit_bytes=8 << 20),
        cost_estimate=pl.CostEstimate(
            flops=20 * polys * ROWS * columns, transcendentals=0, bytes_accessed=12 * polys * ROWS * columns
        ),
        name="finish",
    )(requests, modulus, part, held, result)


def per_device(digits, keys, requests, rotations, moduli):
    modulus = jnp.broadcast_to(moduli.astype(jnp.float32)[:, None], (digits.shape[2], LANES))
    way = key_switch_pair if lax.axis_size("grp") == 2 else key_switch_any
    return way(digits, keys, requests, rotations, modulus)


def key_switch_any(digits, keys, requests, rotations, modulus):
    groups = lax.axis_size("grp")
    blocks = tuple(range(digits.shape[2] // ROWS))
    slots = tuple(range(CAP))
    tail, resident = products(digits, keys, requests, rotations, modulus, slots, blocks, True)
    parts = [add_tail(resident, shifted(tail, "limb", -1))]
    owners = [(0, slots)]
    for steps in range(1, groups):
        asked = shifted(requests, "grp", steps)
        for slot in slots:
            picked = gather(digits, requests, steps, tuple((slot, block) for block in blocks))
            back = []
            for block in blocks:
                arrived = shifted(picked[block], "grp", steps)
                tail, resident = products(
                    arrived[None], keys, asked, rotations, modulus, (slot,), (block,), False
                )
                back.append(shifted(add_tail(resident, shifted(tail, "limb", -1)), "grp", -steps))
            parts.append(jnp.concatenate(back, axis=2))
            owners.append((steps, (slot,)))
    return sums(parts, tuple(owners), requests, modulus, digits.shape[0], False)[0]


def key_switch_pair(digits, keys, requests, rotations, modulus):
    ciphers = digits.shape[0]
    blocks = tuple(range(digits.shape[2] // ROWS))
    slots = tuple(range(CAP))
    turns = [(slot, block) for slot in slots for block in blocks]
    picked = {turns[0]: gather(digits, requests, 1, (turns[0],), 4)[0]}
    picked.update(zip(turns[1:], gather(digits, requests, 1, tuple(turns[1:]))))
    sent = {}
    for slot, block in turns:
        sent[slot, block] = shifted(picked[slot, block], "grp", 1)
    asked = shifted(requests, "grp", 1)
    tail, resident = products(digits, keys, requests, rotations, modulus, slots, blocks, True)
    arrived = shifted(tail, "limb", -1)
    local = add_tail(resident, arrived)
    result, held = sums([local], ((0, slots),), requests, modulus, ciphers, True)
    back = {}
    for slot, block in turns:
        whole = remote(sent[slot, block], keys, asked, rotations, modulus, slot, block)
        back[slot, block] = shifted(whole, "grp", -1)
    for slot, block in turns:
        result = finish(back[slot, block], held, result, requests, modulus, slot, block)
    return result


def remote(arrived, keys, asked, rotations, modulus, slot, block):
    tail, resident = products(arrived[None], keys, asked, rotations, modulus, (slot,), (block,), False)
    wrapped = shifted(tail, "limb", -1)
    return add_tail(resident, wrapped)


def solution(mesh):
    in_specs = (
        P("grp", None, None, "limb"),
        P("grp", None, None, None, "limb"),
        P("grp", None),
        P(),
        P(),
    )
    out_specs = P("grp", None, None, "limb")
    return jax.shard_map(
        per_device, mesh=mesh, in_specs=in_specs, out_specs=out_specs, check_vma=False
    )
```

```python
import functools

import jax
import jax.numpy as jnp
from jax import lax
from jax.experimental import pallas as pl
from jax.experimental.pallas import tpu as pltpu
from jax.sharding import PartitionSpec as P

RMAX = 256
CAP = 2
WIDEST = 2 * RMAX
LANES = 128
ROWS = 8
SMEM = pl.BlockSpec(memory_space=pltpu.SMEM)
VMEM = pl.BlockSpec(memory_space=pltpu.VMEM)


def shifted(value, axis, steps):
    count = lax.axis_size(axis)
    pairs = [(source, (source + steps) % count) for source in range(count)]
    return lax.ppermute(value, axis, pairs)


def slot_ciphers(requests, ciphers, key_count, owner):
    needed = []
    for cipher in range(ciphers):
        flag = requests[cipher, owner * key_count]
        for key in range(1, key_count):
            flag = flag | requests[cipher, owner * key_count + key]
        needed.append(flag)
    return ranked(needed)


def ranked(needed):
    slots = [jnp.int32(0)] * len(needed)
    rank = jnp.int32(0)
    for want in (1, 0):
        for cipher in range(len(needed)):
            here = needed[cipher] == want
            for slot in range(len(needed)):
                slots[slot] = jnp.where(here & (rank == slot), cipher, slots[slot])
            rank = rank + here.astype(jnp.int32)
    return slots


def group_after(steps, groups):
    return lax.rem(lax.axis_index("grp") + steps, groups)


def gather_kernel(wanted, cuts, steps, groups, requests, digits, *refs):
    outs, sems = refs[: len(wanted)], refs[len(wanted)]
    ciphers, parts, _, columns = digits.shape
    chosen = slot_ciphers(requests, ciphers, requests.shape[1] // groups, group_after(steps, groups))
    width = columns // cuts
    loads = []
    for out, (slot, block) in zip(outs, wanted):
        for part in range(parts):
            for cut in range(cuts):
                at = pl.ds(cut * width, width)
                source = digits.at[chosen[slot], part, pl.ds(block * ROWS, ROWS), at]
                loads.append(pltpu.make_async_copy(source, out.at[part, :, at], sems.at[len(loads)]))
    for load in loads:
        load.start()
    for load in loads:
        load.wait()


def gather(digits, requests, steps, wanted, cuts=1):
    parts, _, columns = digits.shape[1:]
    return pl.pallas_call(
        functools.partial(gather_kernel, wanted, cuts, steps, lax.axis_size("grp")),
        out_shape=[jax.ShapeDtypeStruct((parts, ROWS, columns), jnp.float32)] * len(wanted),
        in_specs=[SMEM, pl.BlockSpec(memory_space=pltpu.HBM)],
        out_specs=[VMEM] * len(wanted),
        scratch_shapes=[pltpu.SemaphoreType.DMA((cuts * parts * len(wanted),))],
        compiler_params=pltpu.CompilerParams(vmem_limit_bytes=4 << 20),
        cost_estimate=pl.CostEstimate(
            flops=0, transcendentals=0, bytes_accessed=8 * len(wanted) * parts * ROWS * columns
        ),
        name="gather",
    )(requests, pltpu.with_memory_space_constraint(digits, pltpu.HBM))


def products_kernel(slots, blocks, local, load, requests, rotations, digits, keys, modulus_ref, tail, resident, *refs):
    key_count, parts, polys, _, columns = keys.shape
    ciphers = requests.shape[0]
    pad = WIDEST // LANES
    tiles = columns // LANES
    rolled = refs[0]
    me = lax.axis_index("grp")
    chosen = slot_ciphers(requests, ciphers, key_count, me)
    first = blocks[0]

    def wanted(key):
        flag = requests[chosen[slots[0]], me * key_count + key]
        for slot in slots[1:]:
            flag = flag | requests[chosen[slot], me * key_count + key]
        return flag > 0

    if load:
        whole, (keys, sems) = keys, refs[1:]
        here = pl.ds(blocks[0] * ROWS, len(blocks) * ROWS)
        first = 0

        def copy(key):
            return pltpu.make_async_copy(whole.at[key, :, :, here], keys.at[key], sems.at[key])

        for key in range(key_count):
            pl.when(wanted(key))(copy(key).start)

    tail[...] = jnp.zeros_like(tail)
    resident[...] = jnp.zeros_like(resident)
    rolled[...] = jnp.zeros_like(rolled)
    lane = lax.broadcasted_iota(jnp.int32, (ROWS, LANES), 1)

    def add_key(key, block):
        rows = pl.ds(pl.multiple_of(block * ROWS, ROWS), ROWS)
        limbs = pl.ds(pl.multiple_of((first + block) * ROWS, ROWS), ROWS)
        amount = 2 * rotations[me * key_count + key]
        skipped = amount // LANES
        within = amount - skipped * LANES
        turn = lax.rem(LANES - within, LANES)
        from_this = lane < LANES - within
        modulus = modulus_ref[pl.ds(pl.multiple_of((blocks[0] + block) * ROWS, ROWS), ROWS), :]
        inverse = 1.0 / modulus
        for place, slot in enumerate(slots):
            source = chosen[slot] if local else place

            @pl.when(requests[chosen[slot], me * key_count + key] > 0)
            def _():
                for poly in range(polys):
                    for tile in range(tiles):
                        at = pl.ds(tile * LANES, LANES)
                        combined = digits[source, 0, rows, at] * keys[key, 0, poly, limbs, at]
                        for part in range(1, parts):
                            combined = combined + digits[source, part, rows, at] * keys[key, part, poly, limbs, at]
                        quotient = jnp.floor(combined * inverse)
                        remainder = combined - quotient * modulus
                        rolled[:, pl.ds((pad + tile) * LANES, LANES)] = pltpu.roll(remainder, turn, 1)
                    for tile in range(pad + tiles):
                        start = pl.multiple_of((skipped + tile) * LANES, LANES)
                        after = pl.multiple_of((skipped + tile + 1) * LANES, LANES)
                        moved = jnp.where(from_this, rolled[:, pl.ds(start, LANES)], rolled[:, pl.ds(after, LANES)])
                        if tile < pad:
                            at = pl.ds(tile * LANES, LANES)
                            tail[place, poly, rows, at] = tail[place, poly, rows, at] + moved
                        else:
                            at = pl.ds((tile - pad) * LANES, LANES)
                            resident[place, poly, rows, at] = resident[place, poly, rows, at] + moved

    def add_step(step, carry):
        key = step // len(blocks)
        block = step - key * len(blocks)
        if load:
            pl.when((block == 0) & wanted(key))(lambda: copy(key).wait())

        add_key(key, block)
        return carry

    lax.fori_loop(0, len(blocks) * key_count, add_step, 0)


def products(digits, keys, requests, rotations, modulus, slots, blocks, local, load):
    key_count, parts, polys, _, columns = keys.shape
    count = len(slots)
    limbs = len(blocks) * ROWS
    pad = WIDEST // LANES
    work = count * key_count * polys * limbs * columns
    scratch = [pltpu.VMEM((ROWS, columns + 2 * pad * LANES + LANES), jnp.float32)]
    if load:
        scratch.append(pltpu.VMEM((key_count, parts, polys, limbs, columns), jnp.float32))
        scratch.append(pltpu.SemaphoreType.DMA((key_count,)))
        keys = pltpu.with_memory_space_constraint(keys, pltpu.HBM)
    return pl.pallas_call(
        functools.partial(products_kernel, slots, blocks, local, load),
        out_shape=[
            jax.ShapeDtypeStruct((count, polys, limbs, WIDEST), jnp.float32),
            jax.ShapeDtypeStruct((count, polys, limbs, columns), jnp.float32),
        ],
        in_specs=[SMEM, SMEM, VMEM, pl.BlockSpec(memory_space=pltpu.HBM) if load else VMEM, VMEM],
        out_specs=[VMEM, VMEM],
        scratch_shapes=scratch,
        compiler_params=pltpu.CompilerParams(vmem_limit_bytes=20 << 20),
        cost_estimate=pl.CostEstimate(
            flops=20 * work,
            transcendentals=0,
            bytes_accessed=4 * (key_count * parts * polys * limbs * columns + count * limbs * columns * (parts + polys)),
        ),
        name="products",
    )(requests, rotations, digits, keys, modulus)


def add_tail_kernel(arrived, held, out):
    columns = held.shape[-1]
    at = pl.ds(columns - WIDEST, WIDEST)
    if columns > WIDEST:
        body = pl.ds(0, columns - WIDEST)
        out[:, :, :, body] = held[:, :, :, body]
    out[:, :, :, at] = held[:, :, :, at] + arrived[: held.shape[0]]


def add_tail(resident, arrived):
    return pl.pallas_call(
        add_tail_kernel,
        out_shape=jax.ShapeDtypeStruct(resident.shape, jnp.float32),
        in_specs=[VMEM, VMEM],
        out_specs=VMEM,
        compiler_params=pltpu.CompilerParams(vmem_limit_bytes=8 << 20),
        name="add_tail",
    )(arrived, resident)


def reduce_mod(amount, modulus):
    quotient = jnp.floor(amount * (1.0 / modulus))
    remainder = amount - quotient * modulus
    remainder = jnp.where(remainder < 0, remainder + modulus, remainder)
    return jnp.where(remainder >= modulus, remainder - modulus, remainder)


def sums_kernel(owners, groups, ciphers, key_count, requests, modulus, *refs):
    parts, out = refs[: len(owners)], refs[len(owners)]
    cipher = pl.program_id(1)
    out[...] = jnp.zeros_like(out)
    for part, (steps, slots) in zip(parts, owners):
        chosen = slot_ciphers(requests, ciphers, key_count, group_after(steps, groups))
        for place, slot in enumerate(slots):

            @pl.when(chosen[slot] == cipher)
            def _():
                out[...] = out[...] + part[place]

    wide = modulus[:, :1]
    out[...] = reduce_mod(out[...], wide) / wide


def sums(parts, owners, requests, modulus, ciphers):
    polys, limbs, columns = parts[0].shape[1:]
    groups = lax.axis_size("grp")
    key_count = requests.shape[1] // groups
    return pl.pallas_call(
        functools.partial(sums_kernel, owners, groups, ciphers, key_count),
        out_shape=jax.ShapeDtypeStruct((ciphers, polys, limbs, columns), jnp.float32),
        grid_spec=pltpu.PrefetchScalarGridSpec(
            num_scalar_prefetch=1,
            grid=(limbs // ROWS, ciphers),
            in_specs=[pl.BlockSpec((ROWS, LANES), lambda block, cipher, *_: (block, 0))]
            + [
                pl.BlockSpec((part.shape[0], polys, ROWS, columns), lambda block, cipher, *_: (0, 0, block, 0))
                for part in parts
            ],
            out_specs=pl.BlockSpec(
                (pl.Squeezed(), polys, ROWS, columns), lambda block, cipher, *_: (cipher, 0, block, 0)
            ),
        ),
        compiler_params=pltpu.CompilerParams(
            dimension_semantics=("arbitrary", "arbitrary"), vmem_limit_bytes=24 << 20
        ),
        name="sums",
    )(requests, modulus, *parts)


def orders_of(requests, groups):
    ciphers, columns = requests.shape
    key_count = columns // groups
    bits = key_count.bit_length()
    asks = requests[...]
    row = lax.broadcasted_iota(jnp.int32, asks.shape, 0)
    owner = lax.broadcasted_iota(jnp.int32, asks.shape, 1) // key_count
    me = group_after(0, groups)
    after = group_after(1, groups)
    place = jnp.where(owner == me, 0, ciphers) + row
    code = jnp.sum(jnp.where((owner == me) | (owner == after), asks << (place * bits), 0))
    flags = [
        ((code >> (place * bits)) & ((1 << bits) - 1) > 0).astype(jnp.int32) for place in range(2 * ciphers)
    ]
    return ranked(flags[:ciphers]), ranked(flags[ciphers:]), flags[:ciphers]


def finish_kernel(ranks, blocks, groups, pieces, tailed, requests, modulus, local, *refs):
    parts, (out, done, sems) = refs[:pieces], refs[-3:]
    tails = refs[pieces] if tailed else None
    polys, _, columns = out.shape[1:]
    ours, theirs, _ = orders_of(requests, groups)
    stores = []
    for at, rank in enumerate(ranks):
        cipher = theirs[rank]
        weights = [jnp.where(ours[slot] == cipher, 1.0, 0.0) for slot in range(CAP)]
        for which, block in enumerate(blocks):
            rows = pl.ds(block * ROWS, ROWS)
            here = pl.ds(which * ROWS, ROWS)
            wide = modulus[rows, :1]
            for poly in range(polys):
                total = local[0, poly, rows, :] * weights[0]
                for slot in range(1, CAP):
                    total = total + local[slot, poly, rows, :] * weights[slot]
                if pieces:
                    total = total + parts[which][0, poly]
                if tailed:
                    last = columns - WIDEST
                    wrapped = total[:, last:] + tails[tails.shape[0] - 1, poly, here, :]
                    done[at, poly, here, pl.ds(0, last)] = reduce_mod(total[:, :last], wide) / wide
                    done[at, poly, here, pl.ds(last, WIDEST)] = reduce_mod(wrapped, wide) / wide
                else:
                    done[at, poly, here, :] = reduce_mod(total, wide) / wide
                stores.append(
                    pltpu.make_async_copy(done.at[at, poly, here], out.at[cipher, poly, rows], sems.at[len(stores)])
                )
                stores[-1].start()
    for store in stores:
        store.wait()


def finish(local, requests, modulus, ciphers, ranks, blocks, parts=(), before=None, tails=None):
    _, polys, _, columns = local.shape
    hbm = pl.BlockSpec(memory_space=pltpu.HBM)
    limbs = modulus.shape[0]
    work = len(ranks) * polys * len(blocks) * ROWS * columns
    more = [*parts] + ([] if tails is None else [tails])
    specs = [VMEM] * (3 + len(more))
    if before is not None:
        more, specs = more + [before], specs + [hbm]
    return pl.pallas_call(
        functools.partial(finish_kernel, ranks, blocks, lax.axis_size("grp"), len(parts), tails is not None),
        out_shape=jax.ShapeDtypeStruct((ciphers, polys, limbs, columns), jnp.float32),
        in_specs=specs,
        out_specs=hbm,
        scratch_shapes=[
            pltpu.VMEM((len(ranks), polys, len(blocks) * ROWS, columns), jnp.float32),
            pltpu.SemaphoreType.DMA((len(ranks) * polys * len(blocks),)),
        ],
        input_output_aliases={} if before is None else {len(specs) - 1: 0},
        compiler_params=pltpu.CompilerParams(vmem_limit_bytes=8 << 20),
        cost_estimate=pl.CostEstimate(flops=20 * work, transcendentals=0, bytes_accessed=12 * work),
        name="finish",
    )(requests, modulus, local, *more)


def per_device(digits, keys, requests, rotations, moduli):
    modulus = jnp.broadcast_to(moduli.astype(jnp.float32)[:, None], (digits.shape[2], LANES))
    way = key_switch_pair if lax.axis_size("grp") == 2 else key_switch_any
    return way(digits, keys, requests, rotations, modulus)


def key_switch_any(digits, keys, requests, rotations, modulus):
    groups = lax.axis_size("grp")
    blocks = tuple(range(digits.shape[2] // ROWS))
    slots = tuple(range(CAP))
    tail, resident = products(digits, keys, requests, rotations, modulus, slots, blocks, True, True)
    parts = [add_tail(resident, shifted(tail, "limb", -1))]
    owners = [(0, slots)]
    for steps in range(1, groups):
        asked = shifted(requests, "grp", steps)
        for slot in slots:
            picked = gather(digits, requests, steps, tuple((slot, block) for block in blocks))
            back = []
            for block in blocks:
                arrived = shifted(picked[block], "grp", steps)
                tail, resident = products(
                    arrived[None], keys, asked, rotations, modulus, (slot,), (block,), False, True
                )
                back.append(shifted(add_tail(resident, shifted(tail, "limb", -1)), "grp", -steps))
            parts.append(jnp.concatenate(back, axis=2))
            owners.append((steps, (slot,)))
    return sums(parts, tuple(owners), requests, modulus, digits.shape[0])


def key_switch_pair(digits, keys, requests, rotations, modulus):
    blocks = tuple(range(digits.shape[2] // ROWS))
    slots = tuple(range(CAP))
    key_count = keys.shape[0]
    both = [(0, 1), (1, 0)]
    turns = [(slot, block) for slot in slots for block in blocks]
    picked = {turns[0]: gather(digits, requests, 1, (turns[0],), 4)[0]}
    picked.update(zip(turns[1:], gather(digits, requests, 1, tuple(turns[1:]))))
    sent = {}
    for block in blocks:
        sent[0, block] = lax.ppermute(picked[0, block], "grp", both)
    asked = shifted(requests, "grp", 1)
    me = lax.axis_index("grp")
    rightward = jnp.where(me == 0, requests, asked)[:, key_count:]
    leftward = jnp.where(me == 0, asked, requests)[:, :key_count]
    bits = digits.shape[0].bit_length()
    counts = jnp.sum(jnp.max(rightward, axis=1) + (jnp.max(leftward, axis=1) << bits))
    two_right = counts & ((1 << bits) - 1) > 1
    two_left = counts >> bits > 1
    case = jnp.where(two_right == two_left, 0, jnp.where(two_right, 1, 2))
    ahead = joined(*remote(sent[0, 0], keys, asked, rotations, modulus, 0, 0))

    def branch(pairs):
        def run(*operands):
            return exchange((both, pairs), *operands)

        return run

    branches = [branch(pairs) for pairs in (both, [(0, 1)], [(1, 0)])]
    operands = (ahead, [picked[turn] for turn in turns[len(blocks) :]], [sent[0, block] for block in blocks[1:]], digits)
    return lax.switch(case, branches, *operands, keys, requests, asked, rotations, modulus)


def remote(arrived, keys, asked, rotations, modulus, slot, block):
    return products(arrived[None], keys, asked, rotations, modulus, (slot,), (block,), False, slot == 0)


def joined(tail, resident):
    wrapped = shifted(tail, "limb", -1)
    return add_tail(resident, wrapped)


def exchange(pairs, ahead, picked, arrived, digits, keys, requests, asked, rotations, modulus):
    ciphers = requests.shape[0]
    blocks = digits.shape[2] // ROWS
    whole_blocks = tuple(range(blocks))
    one_way = len(pairs[-1]) == 1
    turns = [(slot, block) for slot in range(CAP) for block in range(blocks)]
    sent = dict(zip(turns[1:blocks], arrived))
    for (slot, block), piece in zip(turns[blocks:], picked):
        sent[slot, block] = lax.ppermute(piece, "grp", pairs[slot])
    tail, resident = products(digits, keys, requests, rotations, modulus, tuple(range(CAP)), whole_blocks, True, True)
    back = {}
    late = []
    for turn in turns:
        slot, block = turn
        ways = [(target, source) for source, target in pairs[slot]]
        if turn == turns[0]:
            whole = ahead
        else:
            wrapped, whole = remote(sent[turn], keys, asked, rotations, modulus, slot, block)
            if len(ways) == 2:
                whole = joined(wrapped, whole)
            else:
                late.append(wrapped)
        if len(late) == blocks:
            returned = lax.ppermute(jnp.concatenate(late, axis=2), "grp", ways)
        back[turn] = lax.ppermute(whole, "grp", ways)
    tails = None
    if one_way:
        tails = shifted(jnp.concatenate([tail, returned]), "limb", -1)
        local = add_tail(resident, tails)
    else:
        local = joined(tail, resident)
    result = finish(local, requests, modulus, ciphers, tuple(range(CAP, ciphers)), whole_blocks)
    if one_way:
        for slot in range(CAP):
            pieces = tuple(back[slot, block] for block in range(blocks))
            late = tails if slot == CAP - 1 else None
            result = finish(local, requests, modulus, ciphers, (slot,), whole_blocks, pieces, result, late)
        return result
    for slot, block in turns:
        result = finish(local, requests, modulus, ciphers, (slot,), (block,), (back[slot, block],), result)
    return result


def solution(mesh):
    in_specs = (
        P("grp", None, None, "limb"),
        P("grp", None, None, None, "limb"),
        P("grp", None),
        P(),
        P(),
    )
    out_specs = P("grp", None, None, "limb")
    return jax.shard_map(
        per_device, mesh=mesh, in_specs=in_specs, out_specs=out_specs, check_vma=False
    )
```

```python
import functools

import jax
import jax.numpy as jnp
from jax import lax
from jax.experimental import pallas as pl
from jax.experimental.pallas import tpu as pltpu
from jax.sharding import PartitionSpec as P

RMAX = 256
CAP = 2
WIDEST = 2 * RMAX
LANES = 128
ROWS = 8
SMEM = pl.BlockSpec(memory_space=pltpu.SMEM)
VMEM = pl.BlockSpec(memory_space=pltpu.VMEM)


def shifted(value, axis, steps):
    count = lax.axis_size(axis)
    pairs = [(source, (source + steps) % count) for source in range(count)]
    return lax.ppermute(value, axis, pairs)


def slot_ciphers(requests, ciphers, key_count, owner):
    needed = []
    for cipher in range(ciphers):
        flag = requests[cipher, owner * key_count]
        for key in range(1, key_count):
            flag = flag | requests[cipher, owner * key_count + key]
        needed.append(flag)
    return ranked(needed)


def ranked(needed):
    slots = [jnp.int32(0)] * len(needed)
    rank = jnp.int32(0)
    for want in (1, 0):
        for cipher in range(len(needed)):
            here = needed[cipher] == want
            for slot in range(len(needed)):
                slots[slot] = jnp.where(here & (rank == slot), cipher, slots[slot])
            rank = rank + here.astype(jnp.int32)
    return slots


def group_after(steps, groups):
    return lax.rem(lax.axis_index("grp") + steps, groups)


def gather_kernel(wanted, cuts, steps, groups, requests, digits, *refs):
    outs, sems = refs[: len(wanted)], refs[len(wanted)]
    ciphers, parts, _, columns = digits.shape
    chosen = slot_ciphers(requests, ciphers, requests.shape[1] // groups, group_after(steps, groups))
    width = columns // cuts
    loads = []
    for out, (slot, block) in zip(outs, wanted):
        for part in range(parts):
            for cut in range(cuts):
                at = pl.ds(cut * width, width)
                source = digits.at[chosen[slot], part, pl.ds(block * ROWS, ROWS), at]
                loads.append(pltpu.make_async_copy(source, out.at[part, :, at], sems.at[len(loads)]))
    for load in loads:
        load.start()
    for load in loads:
        load.wait()


def gather(digits, requests, steps, wanted, cuts=1):
    parts, _, columns = digits.shape[1:]
    return pl.pallas_call(
        functools.partial(gather_kernel, wanted, cuts, steps, lax.axis_size("grp")),
        out_shape=[jax.ShapeDtypeStruct((parts, ROWS, columns), jnp.float32)] * len(wanted),
        in_specs=[SMEM, pl.BlockSpec(memory_space=pltpu.HBM)],
        out_specs=[VMEM] * len(wanted),
        scratch_shapes=[pltpu.SemaphoreType.DMA((cuts * parts * len(wanted),))],
        compiler_params=pltpu.CompilerParams(vmem_limit_bytes=4 << 20),
        cost_estimate=pl.CostEstimate(
            flops=0, transcendentals=0, bytes_accessed=8 * len(wanted) * parts * ROWS * columns
        ),
        name="gather",
    )(requests, pltpu.with_memory_space_constraint(digits, pltpu.HBM))


def products_kernel(slots, blocks, local, load, requests, rotations, digits, keys, modulus_ref, tail, resident, *refs):
    key_count, parts, polys, _, columns = keys.shape
    ciphers = requests.shape[0]
    pad = WIDEST // LANES
    tiles = columns // LANES
    rolled = refs[0]
    me = lax.axis_index("grp")
    chosen = slot_ciphers(requests, ciphers, key_count, me)
    first = blocks[0]

    def wanted(key):
        flag = requests[chosen[slots[0]], me * key_count + key]
        for slot in slots[1:]:
            flag = flag | requests[chosen[slot], me * key_count + key]
        return flag > 0

    if load:
        whole, (keys, sems) = keys, refs[1:]
        here = pl.ds(blocks[0] * ROWS, len(blocks) * ROWS)
        first = 0

        def copy(key):
            return pltpu.make_async_copy(whole.at[key, :, :, here], keys.at[key], sems.at[key])

        for key in range(key_count):
            pl.when(wanted(key))(copy(key).start)

    tail[...] = jnp.zeros_like(tail)
    resident[...] = jnp.zeros_like(resident)
    rolled[...] = jnp.zeros_like(rolled)
    lane = lax.broadcasted_iota(jnp.int32, (ROWS, LANES), 1)

    def add_key(key, block):
        rows = pl.ds(pl.multiple_of(block * ROWS, ROWS), ROWS)
        limbs = pl.ds(pl.multiple_of((first + block) * ROWS, ROWS), ROWS)
        amount = 2 * rotations[me * key_count + key]
        skipped = amount // LANES
        within = amount - skipped * LANES
        turn = lax.rem(LANES - within, LANES)
        from_this = lane < LANES - within
        modulus = modulus_ref[pl.ds(pl.multiple_of((blocks[0] + block) * ROWS, ROWS), ROWS), :]
        inverse = 1.0 / modulus
        for place, slot in enumerate(slots):
            source = chosen[slot] if local else place

            @pl.when(requests[chosen[slot], me * key_count + key] > 0)
            def _():
                for poly in range(polys):
                    for tile in range(tiles):
                        at = pl.ds(tile * LANES, LANES)
                        combined = digits[source, 0, rows, at] * keys[key, 0, poly, limbs, at]
                        for part in range(1, parts):
                            combined = combined + digits[source, part, rows, at] * keys[key, part, poly, limbs, at]
                        quotient = jnp.floor(combined * inverse)
                        remainder = combined - quotient * modulus
                        rolled[:, pl.ds((pad + tile) * LANES, LANES)] = pltpu.roll(remainder, turn, 1)
                    for tile in range(pad + tiles):
                        start = pl.multiple_of((skipped + tile) * LANES, LANES)
                        after = pl.multiple_of((skipped + tile + 1) * LANES, LANES)
                        moved = jnp.where(from_this, rolled[:, pl.ds(start, LANES)], rolled[:, pl.ds(after, LANES)])
                        if tile < pad:
                            at = pl.ds(tile * LANES, LANES)
                            tail[place, poly, rows, at] = tail[place, poly, rows, at] + moved
                        else:
                            at = pl.ds((tile - pad) * LANES, LANES)
                            resident[place, poly, rows, at] = resident[place, poly, rows, at] + moved

    def add_step(step, carry):
        key = step // len(blocks)
        block = step - key * len(blocks)
        if load:
            pl.when((block == 0) & wanted(key))(lambda: copy(key).wait())

        add_key(key, block)
        return carry

    lax.fori_loop(0, len(blocks) * key_count, add_step, 0)


def products(digits, keys, requests, rotations, modulus, slots, blocks, local, load):
    key_count, parts, polys, _, columns = keys.shape
    count = len(slots)
    limbs = len(blocks) * ROWS
    pad = WIDEST // LANES
    work = count * key_count * polys * limbs * columns
    scratch = [pltpu.VMEM((ROWS, columns + 2 * pad * LANES + LANES), jnp.float32)]
    if load:
        scratch.append(pltpu.VMEM((key_count, parts, polys, limbs, columns), jnp.float32))
        scratch.append(pltpu.SemaphoreType.DMA((key_count,)))
        keys = pltpu.with_memory_space_constraint(keys, pltpu.HBM)
    return pl.pallas_call(
        functools.partial(products_kernel, slots, blocks, local, load),
        out_shape=[
            jax.ShapeDtypeStruct((count, polys, limbs, WIDEST), jnp.float32),
            jax.ShapeDtypeStruct((count, polys, limbs, columns), jnp.float32),
        ],
        in_specs=[SMEM, SMEM, VMEM, pl.BlockSpec(memory_space=pltpu.HBM) if load else VMEM, VMEM],
        out_specs=[VMEM, VMEM],
        scratch_shapes=scratch,
        compiler_params=pltpu.CompilerParams(vmem_limit_bytes=20 << 20),
        cost_estimate=pl.CostEstimate(
            flops=20 * work,
            transcendentals=0,
            bytes_accessed=4 * (key_count * parts * polys * limbs * columns + count * limbs * columns * (parts + polys)),
        ),
        name="products",
    )(requests, rotations, digits, keys, modulus)


def add_tail_kernel(arrived, held, out):
    columns = held.shape[-1]
    at = pl.ds(columns - WIDEST, WIDEST)
    if columns > WIDEST:
        body = pl.ds(0, columns - WIDEST)
        out[:, :, :, body] = held[:, :, :, body]
    out[:, :, :, at] = held[:, :, :, at] + arrived[...]


def add_tail(resident, arrived):
    return pl.pallas_call(
        add_tail_kernel,
        out_shape=jax.ShapeDtypeStruct(resident.shape, jnp.float32),
        in_specs=[VMEM, VMEM],
        out_specs=VMEM,
        compiler_params=pltpu.CompilerParams(vmem_limit_bytes=8 << 20),
        name="add_tail",
    )(arrived, resident)


def reduce_mod(amount, modulus):
    quotient = jnp.floor(amount * (1.0 / modulus))
    remainder = amount - quotient * modulus
    remainder = jnp.where(remainder < 0, remainder + modulus, remainder)
    return jnp.where(remainder >= modulus, remainder - modulus, remainder)


def sums_kernel(owners, groups, ciphers, key_count, requests, modulus, *refs):
    parts, out = refs[: len(owners)], refs[len(owners)]
    cipher = pl.program_id(1)
    out[...] = jnp.zeros_like(out)
    for part, (steps, slots) in zip(parts, owners):
        chosen = slot_ciphers(requests, ciphers, key_count, group_after(steps, groups))
        for place, slot in enumerate(slots):

            @pl.when(chosen[slot] == cipher)
            def _():
                out[...] = out[...] + part[place]

    wide = modulus[:, :1]
    out[...] = reduce_mod(out[...], wide) / wide


def sums(parts, owners, requests, modulus, ciphers):
    polys, limbs, columns = parts[0].shape[1:]
    groups = lax.axis_size("grp")
    key_count = requests.shape[1] // groups
    return pl.pallas_call(
        functools.partial(sums_kernel, owners, groups, ciphers, key_count),
        out_shape=jax.ShapeDtypeStruct((ciphers, polys, limbs, columns), jnp.float32),
        grid_spec=pltpu.PrefetchScalarGridSpec(
            num_scalar_prefetch=1,
            grid=(limbs // ROWS, ciphers),
            in_specs=[pl.BlockSpec((ROWS, LANES), lambda block, cipher, *_: (block, 0))]
            + [
                pl.BlockSpec((part.shape[0], polys, ROWS, columns), lambda block, cipher, *_: (0, 0, block, 0))
                for part in parts
            ],
            out_specs=pl.BlockSpec(
                (pl.Squeezed(), polys, ROWS, columns), lambda block, cipher, *_: (cipher, 0, block, 0)
            ),
        ),
        compiler_params=pltpu.CompilerParams(
            dimension_semantics=("arbitrary", "arbitrary"), vmem_limit_bytes=24 << 20
        ),
        name="sums",
    )(requests, modulus, *parts)


def orders_of(requests, groups):
    ciphers, columns = requests.shape
    key_count = columns // groups
    bits = key_count.bit_length()
    asks = requests[...]
    row = lax.broadcasted_iota(jnp.int32, asks.shape, 0)
    owner = lax.broadcasted_iota(jnp.int32, asks.shape, 1) // key_count
    me = group_after(0, groups)
    after = group_after(1, groups)
    place = jnp.where(owner == me, 0, ciphers) + row
    code = jnp.sum(jnp.where((owner == me) | (owner == after), asks << (place * bits), 0))
    flags = [
        ((code >> (place * bits)) & ((1 << bits) - 1) > 0).astype(jnp.int32) for place in range(2 * ciphers)
    ]
    return ranked(flags[:ciphers]), ranked(flags[ciphers:]), flags[:ciphers]


def finish_kernel(ranks, blocks, groups, pieces, tailed, requests, modulus, local, *refs):
    parts, (out, done, sems) = refs[:pieces], refs[-3:]
    tails = refs[pieces] if tailed else None
    polys, _, columns = out.shape[1:]
    ours, theirs, _ = orders_of(requests, groups)
    stores = []
    for at, rank in enumerate(ranks):
        cipher = theirs[rank]
        weights = [jnp.where(ours[slot] == cipher, 1.0, 0.0) for slot in range(CAP)]
        for which, block in enumerate(blocks):
            rows = pl.ds(block * ROWS, ROWS)
            here = pl.ds(which * ROWS, ROWS)
            wide = modulus[rows, :1]
            for poly in range(polys):
                total = local[0, poly, rows, :] * weights[0]
                for slot in range(1, CAP):
                    total = total + local[slot, poly, rows, :] * weights[slot]
                if pieces:
                    total = total + parts[which][0, poly]
                if tailed:
                    last = columns - WIDEST
                    wrapped = total[:, last:] + tails[0, poly, here, :]
                    done[at, poly, here, pl.ds(0, last)] = reduce_mod(total[:, :last], wide) / wide
                    done[at, poly, here, pl.ds(last, WIDEST)] = reduce_mod(wrapped, wide) / wide
                else:
                    done[at, poly, here, :] = reduce_mod(total, wide) / wide
                stores.append(
                    pltpu.make_async_copy(done.at[at, poly, here], out.at[cipher, poly, rows], sems.at[len(stores)])
                )
                stores[-1].start()
    for store in stores:
        store.wait()


def finish(local, requests, modulus, ciphers, ranks, blocks, parts=(), before=None, tails=None):
    _, polys, _, columns = local.shape
    hbm = pl.BlockSpec(memory_space=pltpu.HBM)
    limbs = modulus.shape[0]
    work = len(ranks) * polys * len(blocks) * ROWS * columns
    more = [*parts] + ([] if tails is None else [tails])
    specs = [VMEM] * (3 + len(more))
    if before is not None:
        more, specs = more + [before], specs + [hbm]
    return pl.pallas_call(
        functools.partial(finish_kernel, ranks, blocks, lax.axis_size("grp"), len(parts), tails is not None),
        out_shape=jax.ShapeDtypeStruct((ciphers, polys, limbs, columns), jnp.float32),
        in_specs=specs,
        out_specs=hbm,
        scratch_shapes=[
            pltpu.VMEM((len(ranks), polys, len(blocks) * ROWS, columns), jnp.float32),
            pltpu.SemaphoreType.DMA((len(ranks) * polys * len(blocks),)),
        ],
        input_output_aliases={} if before is None else {len(specs) - 1: 0},
        compiler_params=pltpu.CompilerParams(vmem_limit_bytes=8 << 20),
        cost_estimate=pl.CostEstimate(flops=20 * work, transcendentals=0, bytes_accessed=12 * work),
        name="finish",
    )(requests, modulus, local, *more)


def per_device(digits, keys, requests, rotations, moduli):
    modulus = jnp.broadcast_to(moduli.astype(jnp.float32)[:, None], (digits.shape[2], LANES))
    way = key_switch_pair if lax.axis_size("grp") == 2 else key_switch_any
    return way(digits, keys, requests, rotations, modulus)


def key_switch_any(digits, keys, requests, rotations, modulus):
    groups = lax.axis_size("grp")
    blocks = tuple(range(digits.shape[2] // ROWS))
    slots = tuple(range(CAP))
    tail, resident = products(digits, keys, requests, rotations, modulus, slots, blocks, True, True)
    parts = [add_tail(resident, shifted(tail, "limb", -1))]
    owners = [(0, slots)]
    for steps in range(1, groups):
        asked = shifted(requests, "grp", steps)
        for slot in slots:
            picked = gather(digits, requests, steps, tuple((slot, block) for block in blocks))
            back = []
            for block in blocks:
                arrived = shifted(picked[block], "grp", steps)
                tail, resident = products(
                    arrived[None], keys, asked, rotations, modulus, (slot,), (block,), False, True
                )
                back.append(shifted(add_tail(resident, shifted(tail, "limb", -1)), "grp", -steps))
            parts.append(jnp.concatenate(back, axis=2))
            owners.append((steps, (slot,)))
    return sums(parts, tuple(owners), requests, modulus, digits.shape[0])


def key_switch_pair(digits, keys, requests, rotations, modulus):
    blocks = tuple(range(digits.shape[2] // ROWS))
    slots = tuple(range(CAP))
    key_count = keys.shape[0]
    both = [(0, 1), (1, 0)]
    turns = [(slot, block) for slot in slots for block in blocks]
    picked = {turns[0]: gather(digits, requests, 1, (turns[0],), 4)[0]}
    picked.update(zip(turns[1:], gather(digits, requests, 1, tuple(turns[1:]))))
    sent = {}
    for block in blocks:
        sent[0, block] = lax.ppermute(picked[0, block], "grp", both)
    asked = shifted(requests, "grp", 1)
    me = lax.axis_index("grp")
    rightward = jnp.where(me == 0, requests, asked)[:, key_count:]
    leftward = jnp.where(me == 0, asked, requests)[:, :key_count]
    bits = digits.shape[0].bit_length()
    counts = jnp.sum(jnp.max(rightward, axis=1) + (jnp.max(leftward, axis=1) << bits))
    two_right = counts & ((1 << bits) - 1) > 1
    two_left = counts >> bits > 1
    case = jnp.where(two_right == two_left, 0, jnp.where(two_right, 1, 2))
    ahead = joined(*remote(sent[0, 0], keys, asked, rotations, modulus, 0, 0))

    def branch(pairs):
        def run(*operands):
            return exchange((both, pairs), *operands)

        return run

    branches = [branch(pairs) for pairs in (both, [(0, 1)], [(1, 0)])]
    operands = (ahead, [picked[turn] for turn in turns[len(blocks) :]], [sent[0, block] for block in blocks[1:]], digits)
    return lax.switch(case, branches, *operands, keys, requests, asked, rotations, modulus)


def remote(arrived, keys, asked, rotations, modulus, slot, block):
    return products(arrived[None], keys, asked, rotations, modulus, (slot,), (block,), False, slot == 0)


def joined(tail, resident):
    wrapped = shifted(tail, "limb", -1)
    return add_tail(resident, wrapped)


def exchange(pairs, ahead, picked, arrived, digits, keys, requests, asked, rotations, modulus):
    ciphers = requests.shape[0]
    blocks = digits.shape[2] // ROWS
    whole_blocks = tuple(range(blocks))
    one_way = len(pairs[-1]) == 1
    turns = [(slot, block) for slot in range(CAP) for block in range(blocks)]
    sent = dict(zip(turns[1:blocks], arrived))
    for (slot, block), piece in zip(turns[blocks:], picked):
        sent[slot, block] = lax.ppermute(piece, "grp", pairs[slot])
    tail, resident = products(digits, keys, requests, rotations, modulus, tuple(range(CAP)), whole_blocks, True, True)
    back = {}
    late = []
    for turn in turns:
        slot, block = turn
        ways = [(target, source) for source, target in pairs[slot]]
        if turn == turns[0]:
            whole = ahead
        else:
            wrapped, whole = remote(sent[turn], keys, asked, rotations, modulus, slot, block)
            if len(ways) == 2:
                whole = joined(wrapped, whole)
            else:
                late.append(wrapped)
        if len(late) == blocks:
            returned = lax.ppermute(jnp.concatenate(late, axis=2), "grp", ways)
        back[turn] = lax.ppermute(whole, "grp", ways)
    tails = None
    if one_way:
        tails = shifted(returned, "limb", -1)
    local = joined(tail, resident)
    result = finish(local, requests, modulus, ciphers, tuple(range(CAP, ciphers)), whole_blocks)
    if one_way:
        for slot in range(CAP):
            pieces = tuple(back[slot, block] for block in range(blocks))
            late = tails if slot == CAP - 1 else None
            result = finish(local, requests, modulus, ciphers, (slot,), whole_blocks, pieces, result, late)
        return result
    for slot, block in turns:
        result = finish(local, requests, modulus, ciphers, (slot,), (block,), (back[slot, block],), result)
    return result


def solution(mesh):
    in_specs = (
        P("grp", None, None, "limb"),
        P("grp", None, None, None, "limb"),
        P("grp", None),
        P(),
        P(),
    )
    out_specs = P("grp", None, None, "limb")
    return jax.shard_map(
        per_device, mesh=mesh, in_specs=in_specs, out_specs=out_specs, check_vma=False
    )
```

```python
import functools

import jax
import jax.numpy as jnp
from jax import lax
from jax.experimental import pallas as pl
from jax.experimental.pallas import tpu as pltpu
from jax.sharding import PartitionSpec as P

RMAX = 256
CAP = 2
WIDEST = 2 * RMAX
LANES = 128
ROWS = 8
SMEM = pl.BlockSpec(memory_space=pltpu.SMEM)
VMEM = pl.BlockSpec(memory_space=pltpu.VMEM)


def shifted(value, axis, steps):
    count = lax.axis_size(axis)
    pairs = [(source, (source + steps) % count) for source in range(count)]
    return lax.ppermute(value, axis, pairs)


def slot_ciphers(requests, ciphers, key_count, owner):
    needed = []
    for cipher in range(ciphers):
        flag = requests[cipher, owner * key_count]
        for key in range(1, key_count):
            flag = flag | requests[cipher, owner * key_count + key]
        needed.append(flag)
    return ranked(needed)


def ranked(needed):
    slots = [jnp.int32(0)] * CAP
    rank = jnp.int32(0)
    for want in (1, 0):
        for cipher in range(len(needed)):
            here = needed[cipher] == want
            for slot in range(CAP):
                slots[slot] = jnp.where(here & (rank == slot), cipher, slots[slot])
            rank = rank + here.astype(jnp.int32)
    return slots


def group_after(steps, groups):
    return lax.rem(lax.axis_index("grp") + steps, groups)


def gather_kernel(wanted, cuts, steps, groups, requests, digits, *refs):
    outs, sems = refs[: len(wanted)], refs[len(wanted)]
    ciphers, parts, _, columns = digits.shape
    chosen = slot_ciphers(requests, ciphers, requests.shape[1] // groups, group_after(steps, groups))
    width = columns // cuts
    loads = []
    for out, (slot, block) in zip(outs, wanted):
        for part in range(parts):
            for cut in range(cuts):
                at = pl.ds(cut * width, width)
                source = digits.at[chosen[slot], part, pl.ds(block * ROWS, ROWS), at]
                loads.append(pltpu.make_async_copy(source, out.at[part, :, at], sems.at[len(loads)]))
    for load in loads:
        load.start()
    for load in loads:
        load.wait()


def gather(digits, requests, steps, wanted, cuts=1):
    parts, _, columns = digits.shape[1:]
    return pl.pallas_call(
        functools.partial(gather_kernel, wanted, cuts, steps, lax.axis_size("grp")),
        out_shape=[jax.ShapeDtypeStruct((parts, ROWS, columns), jnp.float32)] * len(wanted),
        in_specs=[SMEM, pl.BlockSpec(memory_space=pltpu.HBM)],
        out_specs=[VMEM] * len(wanted),
        scratch_shapes=[pltpu.SemaphoreType.DMA((cuts * parts * len(wanted),))],
        compiler_params=pltpu.CompilerParams(vmem_limit_bytes=4 << 20),
        cost_estimate=pl.CostEstimate(
            flops=0, transcendentals=0, bytes_accessed=8 * len(wanted) * parts * ROWS * columns
        ),
        name="gather_digits",
    )(*(pltpu.with_memory_space_constraint(array, pltpu.HBM) for array in (requests, digits)))


def products_kernel(slots, blocks, local, requests, rotations, digits, keys, modulus_ref, tail, resident, rolled):
    key_count, parts, polys, _, columns = keys.shape
    ciphers = requests.shape[0]
    pad = WIDEST // LANES
    tiles = columns // LANES
    tail[...] = jnp.zeros_like(tail)
    resident[...] = jnp.zeros_like(resident)
    rolled[...] = jnp.zeros_like(rolled)
    lane = lax.broadcasted_iota(jnp.int32, (ROWS, LANES), 1)
    me = lax.axis_index("grp")
    chosen = slot_ciphers(requests, ciphers, key_count, me)

    def add_key(step, carry):
        block = step // key_count
        key = step - block * key_count
        rows = pl.ds(pl.multiple_of(block * ROWS, ROWS), ROWS)
        limbs = pl.ds(pl.multiple_of((blocks[0] + block) * ROWS, ROWS), ROWS)
        amount = 2 * rotations[me * key_count + key]
        skipped = amount // LANES
        within = amount - skipped * LANES
        turn = lax.rem(LANES - within, LANES)
        from_this = lane < LANES - within
        modulus = modulus_ref[limbs, :]
        inverse = 1.0 / modulus
        for place, slot in enumerate(slots):
            source = chosen[slot] if local else place

            @pl.when(requests[chosen[slot], me * key_count + key] > 0)
            def _():
                for poly in range(polys):
                    for tile in range(tiles):
                        at = pl.ds(tile * LANES, LANES)
                        combined = digits[source, 0, rows, at] * keys[key, 0, poly, limbs, at]
                        for part in range(1, parts):
                            combined = combined + digits[source, part, rows, at] * keys[key, part, poly, limbs, at]
                        quotient = jnp.floor(combined * inverse)
                        remainder = combined - quotient * modulus
                        rolled[:, pl.ds((pad + tile) * LANES, LANES)] = pltpu.roll(remainder, turn, 1)
                    for tile in range(pad + tiles):
                        start = pl.multiple_of((skipped + tile) * LANES, LANES)
                        after = pl.multiple_of((skipped + tile + 1) * LANES, LANES)
                        moved = jnp.where(from_this, rolled[:, pl.ds(start, LANES)], rolled[:, pl.ds(after, LANES)])
                        if tile < pad:
                            at = pl.ds(tile * LANES, LANES)
                            tail[place, poly, rows, at] = tail[place, poly, rows, at] + moved
                        else:
                            at = pl.ds((tile - pad) * LANES, LANES)
                            resident[place, poly, rows, at] = resident[place, poly, rows, at] + moved
        return carry

    lax.fori_loop(0, len(blocks) * key_count, add_key, 0)


def products(digits, keys, requests, rotations, modulus, slots, blocks, local):
    key_count, parts, polys, _, columns = keys.shape
    count = len(slots)
    limbs = len(blocks) * ROWS
    pad = WIDEST // LANES
    work = count * key_count * polys * limbs * columns
    return pl.pallas_call(
        functools.partial(products_kernel, slots, blocks, local),
        out_shape=[
            jax.ShapeDtypeStruct((count, polys, limbs, WIDEST), jnp.float32),
            jax.ShapeDtypeStruct((count, polys, limbs, columns), jnp.float32),
        ],
        in_specs=[SMEM, SMEM, VMEM, VMEM, VMEM],
        out_specs=[VMEM, VMEM],
        scratch_shapes=[pltpu.VMEM((ROWS, columns + 2 * pad * LANES + LANES), jnp.float32)],
        compiler_params=pltpu.CompilerParams(vmem_limit_bytes=20 << 20),
        cost_estimate=pl.CostEstimate(
            flops=20 * work, transcendentals=0, bytes_accessed=4 * (key_count * parts * polys * limbs * columns + count * limbs * columns * (parts + polys))
        ),
        name="products",
    )(requests, rotations, digits, keys, modulus)


def add_tail_kernel(arrived, held, out):
    columns = held.shape[-1]
    at = pl.ds(columns - WIDEST, WIDEST)
    if columns > WIDEST:
        body = pl.ds(0, columns - WIDEST)
        out[:, :, :, body] = held[:, :, :, body]
    out[:, :, :, at] = held[:, :, :, at] + arrived[...]


def add_tail(resident, arrived):
    return pl.pallas_call(
        add_tail_kernel,
        out_shape=jax.ShapeDtypeStruct(resident.shape, jnp.float32),
        in_specs=[VMEM, VMEM],
        out_specs=VMEM,
        compiler_params=pltpu.CompilerParams(vmem_limit_bytes=8 << 20),
        name="add_tail",
    )(arrived, resident)


def reduce_mod(amount, modulus):
    quotient = jnp.floor(amount * (1.0 / modulus))
    remainder = amount - quotient * modulus
    remainder = jnp.where(remainder < 0, remainder + modulus, remainder)
    return jnp.where(remainder >= modulus, remainder - modulus, remainder)


def sums_kernel(owners, groups, ciphers, key_count, keep, requests, modulus, *refs):
    parts = refs[: len(owners)]
    out = refs[len(owners)]
    cipher = pl.program_id(1)
    out[...] = jnp.zeros_like(out)
    for part, (steps, slots) in zip(parts, owners):
        chosen = slot_ciphers(requests, ciphers, key_count, group_after(steps, groups))
        for place, slot in enumerate(slots):

            @pl.when(chosen[slot] == cipher)
            def _():
                out[...] = out[...] + part[place]

    if keep:
        held = refs[len(owners) + 1]
        chosen = slot_ciphers(requests, ciphers, key_count, group_after(groups - 1, groups))
        for slot in range(CAP):

            @pl.when(chosen[slot] == cipher)
            def _():
                held[slot] = out[...]

    wide = modulus[:, :1]
    out[...] = reduce_mod(out[...], wide) / wide


def sums(parts, owners, requests, modulus, ciphers, keep):
    polys, limbs, columns = parts[0].shape[1:]
    groups = lax.axis_size("grp")
    key_count = requests.shape[1] // groups
    shapes = [jax.ShapeDtypeStruct((ciphers, polys, limbs, columns), jnp.float32)]
    specs = [pl.BlockSpec((pl.Squeezed(), polys, ROWS, columns), lambda block, cipher, *_: (cipher, 0, block, 0))]
    if keep:
        shapes.append(jax.ShapeDtypeStruct((CAP, polys, limbs, columns), jnp.float32))
        specs.append(pl.BlockSpec((CAP, polys, ROWS, columns), lambda block, cipher, *_: (0, 0, block, 0)))
    return pl.pallas_call(
        functools.partial(sums_kernel, owners, groups, ciphers, key_count, keep),
        out_shape=shapes,
        grid_spec=pltpu.PrefetchScalarGridSpec(
            num_scalar_prefetch=1,
            grid=(limbs // ROWS, ciphers),
            in_specs=[pl.BlockSpec((ROWS, LANES), lambda block, cipher, *_: (block, 0))]
            + [
                pl.BlockSpec((part.shape[0], polys, ROWS, columns), lambda block, cipher, *_: (0, 0, block, 0))
                for part in parts
            ],
            out_specs=specs,
        ),
        compiler_params=pltpu.CompilerParams(
            dimension_semantics=("arbitrary", "arbitrary"), vmem_limit_bytes=24 << 20
        ),
        cost_estimate=pl.CostEstimate(
            flops=20 * ciphers * polys * limbs * columns,
            transcendentals=0,
            bytes_accessed=4 * (ciphers + 2 + 2 * len(parts)) * polys * limbs * columns,
        ),
        name="sums",
    )(requests, modulus, *parts)


def finish_kernel(slot, block, groups, requests, modulus, part, held, before, out, done, sems):
    ciphers, polys, _, _ = out.shape
    key_count = requests.shape[1] // groups
    rows = pl.ds(block * ROWS, ROWS)
    wide = modulus[rows, :1]
    for poly in range(polys):
        done[poly] = reduce_mod(held[slot, poly, rows, :] + part[0, poly], wide) / wide
    asks = requests[...]
    column = lax.broadcasted_iota(jnp.int32, asks.shape, 1) // key_count
    row = lax.broadcasted_iota(jnp.int32, asks.shape, 0)
    asks = jnp.where(column == group_after(groups - 1, groups), asks, 0)
    needed = [jnp.max(jnp.where(row == cipher, asks, 0)) for cipher in range(ciphers)]
    cipher = ranked(needed)[slot]
    stores = [
        pltpu.make_async_copy(done.at[poly], out.at[cipher, poly, rows], sems.at[poly]) for poly in range(polys)
    ]
    for store in stores:
        store.start()
    for store in stores:
        store.wait()


def finish(part, held, result, requests, modulus, slot, block):
    _, polys, _, columns = result.shape
    groups = lax.axis_size("grp")
    hbm = pl.BlockSpec(memory_space=pltpu.HBM)
    return pl.pallas_call(
        functools.partial(finish_kernel, slot, block, groups),
        out_shape=jax.ShapeDtypeStruct(result.shape, jnp.float32),
        in_specs=[VMEM, VMEM, VMEM, VMEM, hbm],
        out_specs=hbm,
        scratch_shapes=[pltpu.VMEM((polys, ROWS, columns), jnp.float32), pltpu.SemaphoreType.DMA((polys,))],
        input_output_aliases={4: 0},
        compiler_params=pltpu.CompilerParams(vmem_limit_bytes=8 << 20),
        cost_estimate=pl.CostEstimate(
            flops=20 * polys * ROWS * columns, transcendentals=0, bytes_accessed=12 * polys * ROWS * columns
        ),
        name="finish",
    )(requests, modulus, part, held, result)


def per_device(digits, keys, requests, rotations, moduli):
    modulus = jnp.broadcast_to(moduli.astype(jnp.float32)[:, None], (digits.shape[2], LANES))
    way = key_switch_pair if lax.axis_size("grp") == 2 else key_switch_any
    return way(digits, keys, requests, rotations, modulus)


def key_switch_any(digits, keys, requests, rotations, modulus):
    groups = lax.axis_size("grp")
    blocks = tuple(range(digits.shape[2] // ROWS))
    slots = tuple(range(CAP))
    tail, resident = products(digits, keys, requests, rotations, modulus, slots, blocks, True)
    parts = [add_tail(resident, shifted(tail, "limb", -1))]
    owners = [(0, slots)]
    for steps in range(1, groups):
        asked = shifted(requests, "grp", steps)
        for slot in slots:
            picked = gather(digits, requests, steps, tuple((slot, block) for block in blocks))
            back = []
            for block in blocks:
                arrived = shifted(picked[block], "grp", steps)
                tail, resident = products(
                    arrived[None], keys, asked, rotations, modulus, (slot,), (block,), False
                )
                back.append(shifted(add_tail(resident, shifted(tail, "limb", -1)), "grp", -steps))
            parts.append(jnp.concatenate(back, axis=2))
            owners.append((steps, (slot,)))
    return sums(parts, tuple(owners), requests, modulus, digits.shape[0], False)[0]


def key_switch_pair(digits, keys, requests, rotations, modulus):
    ciphers = digits.shape[0]
    blocks = tuple(range(digits.shape[2] // ROWS))
    slots = tuple(range(CAP))
    turns = [(slot, block) for slot in slots for block in blocks]
    picked = {turns[0]: gather(digits, requests, 1, (turns[0],), 4)[0]}
    picked.update(zip(turns[1:], gather(digits, requests, 1, tuple(turns[1:]))))
    sent = {}
    for slot, block in turns:
        sent[slot, block] = shifted(picked[slot, block], "grp", 1)
    asked = shifted(requests, "grp", 1)
    tail, resident = products(digits, keys, requests, rotations, modulus, slots, blocks, True)
    arrived = shifted(tail, "limb", -1)
    local = add_tail(resident, arrived)
    result, held = sums([local], ((0, slots),), requests, modulus, ciphers, True)
    back = {}
    for slot, block in turns:
        whole = remote(sent[slot, block], keys, asked, rotations, modulus, slot, block)
        back[slot, block] = shifted(whole, "grp", -1)
    for slot, block in turns:
        result = finish(back[slot, block], held, result, requests, modulus, slot, block)
    return result


def remote(arrived, keys, asked, rotations, modulus, slot, block):
    tail, resident = products(arrived[None], keys, asked, rotations, modulus, (slot,), (block,), False)
    wrapped = shifted(tail, "limb", -1)
    return add_tail(resident, wrapped)


def solution(mesh):
    in_specs = (
        P("grp", None, None, "limb"),
        P("grp", None, None, None, "limb"),
        P("grp", None),
        P(),
        P(),
    )
    out_specs = P("grp", None, None, "limb")
    return jax.shard_map(
        per_device, mesh=mesh, in_specs=in_specs, out_specs=out_specs, check_vma=False
    )
```
